128 devices in a mesh: rows: 16 (over y, x), cols: 8 (over z, core).
Axes of the slice: x: 4, y: 4, z: 4, core: 2. Of those that a mesh axis runs over, the one named last changes fastest.
Arguments:
- latent: bfloat16 [512, 512, 320], P('rows', 'cols'), may hold values from -100 to 100
- conv_weights: bfloat16 [5, 2880, 320], P(None, 'rows'), may hold values from -0.109375 to 0.109375
- conv_bias: float32 [5, 320], replicated, may hold values from -4 to 4
- norm_gain: float32 [4, 320], replicated, may hold values from 0.25 to 1.75
- norm_shift: float32 [4, 320], replicated, may hold values from -4 to 4
- time_shift: float32 [2, 320], replicated, may hold values from -5 to 5
Outputs:
- features: bfloat16 [512, 512, 320], P('rows', 'cols')
- reduced: bfloat16 [256, 256, 320], P('rows', 'cols')
The draws below stay inside these ranges and needn't reach their ends.
All inputs are finite; a program needn't handle non-finite values.
Results may differ from the reference program's by a relative error of at most 0.01.
Values may be sent and summed in bfloat16 or wider, within the bound.
A program may use at most 128 MiB of HBM per device.

```python
import jax
import jax.numpy as jnp
from jax import lax

C = 320
GROUPS = 32
H = 512
W = 512


def draw_latent(key, part):
    key_chan = jax.random.fold_in(key, 11)
    key_cell = jax.random.fold_in(key, 12)
    key_vals = jax.random.fold_in(key, 13)
    channel_scale = jnp.exp(jax.random.uniform(key_chan, (C,), jnp.float32, -1.15, 1.15))
    cell_scale = jnp.exp(jax.random.uniform(key_cell, (H, W, 1), jnp.float32, -1.15, 1.15))
    row_pos = jnp.arange(H, dtype=jnp.float32) / H
    col_pos = jnp.arange(W, dtype=jnp.float32) / W
    rise = jnp.exp(jnp.log(3.0) * row_pos[:, None] + jnp.log(1.5) * col_pos[None, :])[:, :, None]
    values = jnp.clip(jax.random.normal(key_vals, (H, W, C), jnp.float32), -4.0, 4.0) + 0.8
    return (values * channel_scale * cell_scale * rise * 0.3).astype(jnp.bfloat16)


def block_levels(own_key, shape, cuts, smallest, top_value):
    def one(position, parts):
        heights = jax.random.uniform(jax.random.fold_in(jax.random.fold_in(own_key, 6), position), (parts,), jnp.float32, smallest / len(cuts), top_value / len(cuts))
        return jnp.repeat(jnp.exp(heights), shape[position] // parts).reshape((-1,) + (1,) * (len(shape) - position - 1))

    level = one(*cuts[0])
    for cut in cuts[1:]:
        level = level * one(*cut)
    return level


def centred(own_key, dims, width, bound, split=(), held_as=jnp.bfloat16):
    factor_of = block_levels(own_key, dims, split, -0.22, 0.18) if split else 1.0
    values = jax.random.normal(own_key, dims, jnp.float32) * width * factor_of
    return jnp.minimum(jnp.maximum(values, -bound), bound).astype(held_as)


def setup_inputs(seed: int = 0) -> dict:
    arg_keys = jax.random.split(jax.random.key(seed), 7)
    return {
        "latent": draw_latent(jax.random.fold_in(arg_keys[6], 71), 0),
        "conv_weights": centred(arg_keys[1], (5, 9 * C, C), (9 * C) ** -0.5, 0.109375, ((1, 16),)),
        "conv_bias": centred(arg_keys[2], (5, C), 0.3, 4.0, (), jnp.float32),
        "norm_gain": jnp.clip(1.0 + 0.15 * jax.random.normal(arg_keys[3], (4, C), jnp.float32), 0.25, 1.75),
        "norm_shift": centred(arg_keys[4], (4, C), 0.5, 4.0, (), jnp.float32),
        "time_shift": centred(arg_keys[5], (2, C), 1.0, 5.0, (), jnp.float32),
    }


eps = 1e-05

def group_norm(act, gain, shift):
    values = act.astype(jnp.float32).reshape(H * W, GROUPS, C // GROUPS)
    mean = lax.optimization_barrier(jnp.mean(values, axis=(0, 2)))
    deviate = values - mean[None, :, None]
    spread = lax.optimization_barrier(jnp.mean(deviate * deviate, axis=(0, 2)))
    scaled = deviate * lax.rsqrt(spread + eps)[None, :, None]
    scaled = scaled.reshape(H, W, C) * gain + shift
    return jax.nn.silu(scaled).astype(jnp.bfloat16)

def convolve(act, weight, bias, stride):
    kernel = weight.astype(jnp.float32).reshape(3, 3, C, C)
    result = lax.conv_general_dilated(act.astype(jnp.float32)[None], kernel, (stride, stride), ((1, 1), (1, 1)), dimension_numbers=('NHWC', 'HWIO', 'NHWC'), precision=lax.Precision.HIGHEST)[0]
    return result + bias

def reference(latent, conv_weights, conv_bias, norm_gain, norm_shift, time_shift):
    current = latent
    for block in range(2):
        first = 2 * block
        normed = group_norm(current, norm_gain[first], norm_shift[first])
        inner = (convolve(normed, conv_weights[first], conv_bias[first], 1) + time_shift[block]).astype(jnp.bfloat16)
        normed = group_norm(inner, norm_gain[first + 1], norm_shift[first + 1])
        branch = convolve(normed, conv_weights[first + 1], conv_bias[first + 1], 1)
        current = (current.astype(jnp.float32) + branch).astype(jnp.bfloat16)
    reduced = convolve(current, conv_weights[4], conv_bias[4], 2).astype(jnp.bfloat16)
    return (current, reduced)
```

```python
import functools

import jax
import jax.numpy as jnp
from jax import lax
from jax.experimental import pallas as pl
from jax.experimental.pallas import tpu as pltpu
from jax.sharding import Mesh
from jax.sharding import PartitionSpec as P

f32, bf16 = jnp.float32, jnp.bfloat16
MESH = pl.DeviceIdType.MESH
ROWS = ("rows_0", "rows_1")
COLS = ("cols_0", "cols_1")
NY, NX, NZ, NC = 4, 4, 4, 2
NR, NCOL = NY * NX, NZ * NC
C = 320
TH, TW = 32, 64
SHARD = 180
RB = 16
EPS = 1e-05


def padded(row, width=384):
    return jnp.concatenate([row, jnp.zeros((row.shape[0], width - row.shape[1]), row.dtype)], axis=1)


def window_tiles():
    tiles = []
    for tile in range(9 * C // 16):
        holders = []
        for r in range(NR):
            first = SHARD * r // 16
            last = (SHARD * (r + 1) - 1) // 16
            if first <= tile <= last:
                holders.append((r, tile - first))
        tiles.append(holders)
    return tiles


WINDOWS = window_tiles()


def kernel(
    lat_hbm, w_hbm, bias_ref, gain_ref, shift_ref, time_ref,
    feat_hbm, red_hbm,
    lat, wl, act_a, act_b, xs, r0, edge_mat, zs, ze, hc, es, cs, gath, wk, blockdiag,
    ar_src, ar_a, ar_b, fbuf, rbuf,
    sem_in, sem_out, ws_send, ws_recv, halo_send, halo_recv, ar_send, ar_recv,
):
    y, x = lax.axis_index("rows_0"), lax.axis_index("rows_1")
    z, core = lax.axis_index("cols_0"), lax.axis_index("cols_1")
    r, c = y * NX + x, z * NC + core

    def dev(rr, cc):
        return (rr // NX, lax.rem(rr, NX), cc // NC, lax.rem(cc, NC))

    def row_peer(j):
        return dev(lax.rem(r + j, NR), c)

    def col_peer(j):
        return dev(r, lax.rem(c + j, NCOL))

    up, down = lax.rem(r + NR - 1, NR), lax.rem(r + 1, NR)
    left, right = lax.rem(c + NCOL - 1, NCOL), lax.rem(c + 1, NCOL)

    lat_copies = []
    for i in range(4):
        cp = pltpu.make_async_copy(lat_hbm.at[pl.ds(8 * i, 8)], lat.at[pl.ds(8 * i, 8)], sem_in.at[i])
        cp.start()
        lat_copies.append(cp)
    w_copy = pltpu.make_async_copy(w_hbm, wl, sem_in.at[4])
    w_copy.start()

    barrier = pltpu.get_barrier_semaphore()
    peers = [row_peer(j) for j in range(1, NR)] + [col_peer(j) for j in range(1, NCOL)]
    peers += [dev(up, left), dev(up, right), dev(down, left), dev(down, right)]
    for peer in peers:
        pl.semaphore_signal(barrier, inc=1, device_id=peer, device_id_type=MESH)

    major = jnp.where(core == 0, y, x)
    minor = jnp.where(core == 0, x, y)
    slot = 4 * major + minor
    w_copy.wait()
    off = lax.rem(4 * r, 16)
    row_id = lax.broadcasted_iota(jnp.int32, (96, SHARD), 0) + 96 * core
    col_id = lax.broadcasted_iota(jnp.int32, (96, SHARD), 1) + off
    place = jnp.where(row_id == col_id, 1.0, 0.0).astype(bf16)
    for k in range(5):
        half = jnp.dot(place, wl[k], preferred_element_type=f32)
        gath[k, core, slot, 0:96] = half[:, 0:128].astype(bf16)
        gath[k, core, slot, 96:192] = half[:, 128:256].astype(bf16)
        tail = jnp.concatenate([half[0:48, 256:320], half[48:96, 256:320]], axis=1)
        gath[k, core, slot, 192:240] = tail.astype(bf16)

    pl.semaphore_wait(barrier, len(peers))

    def along(step_minor, step_major):
        mi = lax.rem(minor + step_minor, 4)
        ma = lax.rem(major + step_major, 4)
        return (jnp.where(core == 0, ma, mi), jnp.where(core == 0, mi, ma), z, core)

    pending_sends = []

    def w_stage1(k):
        mine = gath.at[k, core, slot]
        for j in range(1, 4):
            pltpu.make_async_remote_copy(mine, mine, ws_send.at[k, 0], ws_recv.at[k, 0], along(j, 0), MESH).start()
        pending_sends.append((gath.at[k, 0, 0:3], ws_send.at[k, 0]))

    def w_stage2(k):
        three = gath.at[k, 0, 0:3]
        pltpu.make_async_copy(three, three, ws_recv.at[k, 0]).wait()
        mine = gath.at[k, core, pl.ds(4 * major, 4)]
        for j in range(1, 4):
            pltpu.make_async_remote_copy(mine, mine, ws_send.at[k, 1], ws_recv.at[k, 1], along(0, j), MESH).start()
        pending_sends.append((gath.at[k, 0, 0:12], ws_send.at[k, 1]))

    def w_swap(k):
        twelve = gath.at[k, 0, 0:12]
        pltpu.make_async_copy(twelve, twelve, ws_recv.at[k, 1]).wait()
        mine = gath.at[k, core]
        pltpu.make_async_remote_copy(
            mine, mine, ws_send.at[k, 2], ws_recv.at[k, 2], (y, x, z, 1 - core), MESH
        ).start()
        pending_sends.append((gath.at[k, 0], ws_send.at[k, 2]))

    def w_arrived(k):
        every = gath.at[k, 0]
        pltpu.make_async_copy(every, every, ws_recv.at[k, 2]).wait()

    w_stage1(0)

    lane = lax.broadcasted_iota(jnp.int32, (1, 128), 1)
    low = lane < 64

    def relayout(k):
        wbuf = wk.at[k % 2]

        def piece(holder, part):
            rr, l = holder
            h, l6 = l // 6, l % 6
            s = rr if h == 0 else (rr % NX) * NY + rr // NX
            if part < 2:
                return gath[k, h, s, 96 * part + 16 * l6 : 96 * part + 16 * l6 + 16]
            t = gath[k, h, s, 192 + 16 * (l6 % 3) : 208 + 16 * (l6 % 3)].astype(f32)
            return t if l6 < 3 else pltpu.roll(t, 64, 1)

        def tile(t, part):
            return functools.reduce(lambda p, q: p + q, [piece(h, part) for h in WINDOWS[t]])

        for a in range(3):
            for u in range(20):
                row = 256 * a + 16 * u if u < 16 else 768 + 64 * a + 16 * (u - 16)
                tails = []
                for b in range(3):
                    t = 20 * (3 * a + b) + u
                    for part in range(2):
                        wbuf[row : row + 16, 256 * b + 128 * part : 256 * b + 128 * part + 128] = tile(t, part)
                    tails.append(jnp.where(low, tile(t, 2), 0.0))
                wbuf[row : row + 16, 768:896] = (tails[0] + pltpu.roll(tails[1], 64, 1)).astype(bf16)
                wbuf[row : row + 16, 896:1024] = tails[2].astype(bf16)

    for i in range(2):
        wk[i, 960:1024, :] = jnp.zeros((64, 1024), bf16)
    ci = lax.broadcasted_iota(jnp.int32, (384, 384), 0)
    cj = lax.broadcasted_iota(jnp.int32, (384, 384), 1)
    same = ((ci * 6554) >> 16) == ((cj * 6554) >> 16)
    blockdiag[...] = jnp.where(same, 1.0, 0.0).astype(bf16)

    zero_acc = tuple(jnp.zeros((8, 128), f32) for _ in range(6))

    def fold(v):
        return jnp.sum(v.reshape(v.shape[0] // 8, 8, 128), axis=0)

    def add_stats(acc, tiles):
        sums = [acc[t] + fold(tiles[t]) for t in range(3)]
        squares = [acc[3 + t] + fold(tiles[t] * tiles[t]) for t in range(3)]
        return tuple(sums + squares)

    def stage_cols(phase, row, tiles):
        for t in range(3):
            cs[phase, 0, t, pl.ds(row, 1), :] = tiles[t][0:1]
            cs[phase, 1, t, pl.ds(row, 1), :] = tiles[t][63:64]

    def halo_messages(phase, act):
        msgs = [
            (act.at[TH], act.at[0], dev(down, c)),
            (cs.at[phase, 1], hc.at[phase, 0, :, 8:40, :], dev(r, right)),
            (cs.at[phase, 1, :, 24:32, :], hc.at[phase, 0, :, 0:8, :], dev(down, right)),
        ]
        if phase < 4:
            msgs += [
                (act.at[1], act.at[TH + 1], dev(up, c)),
                (cs.at[phase, 0], hc.at[phase, 1, :, 8:40, :], dev(r, left)),
                (cs.at[phase, 0, :, 24:32, :], hc.at[phase, 1, :, 0:8, :], dev(down, left)),
                (cs.at[phase, 1, :, 0:8, :], hc.at[phase, 0, :, 40:48, :], dev(up, right)),
                (cs.at[phase, 0, :, 0:8, :], hc.at[phase, 1, :, 40:48, :], dev(up, left)),
            ]
        return [
            pltpu.make_async_remote_copy(s, d, halo_send.at[phase, i], halo_recv.at[phase, i], to, MESH)
            for i, (s, d, to) in enumerate(msgs)
        ]

    def all_sum(phase, acc, between):
        vec = jnp.concatenate(
            [jnp.sum(v, axis=0, keepdims=True) for v in acc] + [jnp.zeros((2, 128), f32)], axis=0
        )
        for stage, (buf, peer, n) in enumerate(((ar_a, col_peer, NCOL), (ar_b, row_peer, NR))):
            src = ar_src.at[phase, stage]
            src[...] = vec
            for j in range(1, n):
                pltpu.make_async_remote_copy(
                    src, buf.at[phase, j - 1], ar_send.at[phase, stage], ar_recv.at[phase, stage], peer(j), MESH
                ).start()
            pending_sends.append((buf.at[phase], ar_send.at[phase, stage]))
            between[stage]()
            pltpu.make_async_copy(buf.at[phase], buf.at[phase], ar_recv.at[phase, stage]).wait()
            vec = functools.reduce(lambda p, q: p + q, [vec] + [buf[phase, j] for j in range(n - 1)])
        return vec

    def scales(phase, vec):
        both = jnp.concatenate(
            [
                jnp.concatenate([vec[0:1], vec[1:2], vec[2:3]], axis=1),
                jnp.concatenate([vec[3:4], vec[4:5], vec[5:6]], axis=1),
            ],
            axis=0,
        )
        hi = both.astype(bf16).astype(f32)
        mid = (both - hi).astype(bf16).astype(f32)
        lo = both - hi - mid
        parts = jnp.concatenate([hi, mid, lo, jnp.zeros((10, 384), f32)], axis=0).astype(bf16)
        tot = jnp.dot(parts, blockdiag[...], preferred_element_type=f32)
        sums = tot[0:1] + tot[2:3] + tot[4:5]
        squares = tot[1:2] + tot[3:4] + tot[5:6]
        count = float(TH * NR * TW * NCOL * (C // 32))
        mean = sums / count
        spread = jnp.maximum(squares / count - mean * mean, 0.0)
        scale = lax.rsqrt(spread + EPS) * padded(gain_ref[phase : phase + 1, :])
        move = padded(shift_ref[phase : phase + 1, :]) - mean * scale
        scale, move = 0.5 * scale, 0.5 * move
        return [scale[:, 128 * t : 128 * t + 128] for t in range(3)], [move[:, 128 * t : 128 * t + 128] for t in range(3)]

    def silu_of(v, scale, move):
        half = v * scale + move
        return half + half * jnp.tanh(half)

    def on(cond):
        return jnp.where(cond, 1.0, 0.0).astype(f32)

    top, bottom = on(r > 0), on(r < NR - 1)
    west, east = on(c > 0), on(c < NCOL - 1)

    def edges_to_matrix(rows, stride, sides):
        for side in range(sides):
            at = slice(rows * side, rows * side + rows)
            taps = [
                [es[side, t, pl.ds(7 + a, rows, stride=stride) if stride > 1 else pl.ds(7 + a, rows), :] for t in range(3)]
                for a in range(3)
            ]
            for a in range(3):
                for t in range(2):
                    edge_mat[at, 256 * a + 128 * t : 256 * a + 128 * t + 128] = taps[a][t].astype(bf16)
            edge_mat[at, 768:896] = (taps[0][2] + pltpu.roll(taps[1][2], 64, 1)).astype(bf16)
            edge_mat[at, 896:1024] = taps[2][2].astype(bf16)

    er = lax.broadcasted_iota(jnp.int32, (48, 1), 0)
    edge_rows = jnp.where(er < 8, top, jnp.where(er < 40, 1.0, bottom))

    def normalize(phase, act, sc, mv):
        def one(i, prev):
            m = jnp.where(i == 0, top, jnp.where(i == TH + 1, bottom, 1.0))
            tiles = []
            for t in range(3):
                v = act[i, :, 128 * t : 128 * t + 128].astype(f32)
                tiles.append(silu_of(v, sc[t] * m, mv[t] * m))
                xs[i, :, 128 * t : 128 * t + 128] = tiles[t].astype(bf16)
            r0[i, :, :] = (prev + pltpu.roll(tiles[2], 64, 1)).astype(bf16)
            return tiles[2]

        lax.fori_loop(0, TH + 2, one, jnp.zeros((TW, 128), f32))
        for side, mask in ((0, west), (1, east)):
            for t in range(3):
                es[side, t] = silu_of(hc[phase, side, t], sc[t], mv[t]) * (edge_rows * mask)
        edges_to_matrix(TH, 1, 2)

    def edge_dot(k, rows):
        for n in range(4):
            o = jnp.dot(edge_mat[0:rows], wk[k % 2, :, 256 * n : 256 * n + 256], preferred_element_type=f32)
            ze[2 * n, 0:rows] = o[:, 0:128]
            ze[2 * n + 1, 0:rows] = o[:, 128:256]

    def block_dot(k, parts):
        lhs = jnp.concatenate(parts, axis=1)
        for n in range(4):
            o = jnp.dot(lhs, wk[k % 2, :, 256 * n : 256 * n + 256], preferred_element_type=f32)
            zs[2 * n, :, 8 : 8 + TW, :] = o[:, 0:128].reshape(RB, TW, 128)
            zs[2 * n + 1, :, 8 : 8 + TW, :] = o[:, 128:256].reshape(RB, TW, 128)

    def taps_sum(rr, width, stride):
        def at(t, first):
            if stride > 1:
                return zs[t, rr, pl.ds(first, width, stride=stride), :]
            return zs[t, rr, first : first + width, :]

        outs = [at(t, 7) + at(2 + t, 8) + at(4 + t, 9) for t in range(2)]
        tail = at(6, 7) + pltpu.roll(at(6, 8), 64, 1) + at(7, 9)
        return outs + [jnp.where(low, tail, 0.0)]

    def place_edges(rr, row, rows, both):
        for t in (0, 1, 6):
            zs[t, rr, 7:8, :] = ze[t, pl.ds(row, 1), :]
        if both:
            for t in (4, 5, 7):
                zs[t, rr, 72:73, :] = ze[t, pl.ds(rows + row, 1), :]

    def split(row):
        row = padded(row)
        return [row[:, 128 * t : 128 * t + 128] for t in range(3)]

    def convolve(k, res, out):
        extra = split(bias_ref[k : k + 1, :] + (time_ref[k // 2 : k // 2 + 1, :] if k % 2 == 0 else 0.0))
        edge_dot(k, 2 * TH)

        def block(i, acc):
            first = i * RB
            parts = [xs[pl.ds(first + a, RB), :, 0:256].reshape(RB * TW, 256) for a in range(3)]
            parts.append(r0[pl.ds(first + 1, RB)].reshape(RB * TW, 128))
            parts.append(xs[pl.ds(first + 2, RB), :, 256:384].reshape(RB * TW, 128))
            block_dot(k, parts)

            def one(rr, acc):
                row = first + rr
                place_edges(rr, row, TH, True)
                tiles = []
                for t, o in enumerate(taps_sum(rr, TW, 1)):
                    o = o + extra[t]
                    if res is not None:
                        o = o + res[row + 1, :, 128 * t : 128 * t + 128].astype(f32)
                    o = o.astype(bf16)
                    out[row + 1, :, 128 * t : 128 * t + 128] = o
                    tiles.append(o.astype(f32))
                stage_cols(k + 1, row, tiles)
                if k == 3:
                    fbuf[row] = jnp.concatenate([tiles[0], tiles[1], tiles[2][:, 0:64]], axis=1).astype(bf16)
                    return acc
                return add_stats(acc, tiles)

            return lax.fori_loop(0, RB, one, acc)

        return lax.fori_loop(0, TH // RB, block, zero_acc)

    def read_latent(i, acc):
        v = lat[i].astype(f32)
        tiles = [v[:, 0:128], v[:, 128:256], padded(v[:, 256:320], 128)]
        for t in range(3):
            act_a[i + 1, :, 128 * t : 128 * t + 128] = tiles[t].astype(bf16)
        stage_cols(0, i, tiles)
        return add_stats(acc, tiles)

    acc = zero_acc
    for i in range(4):
        lat_copies[i].wait()
        acc = lax.fori_loop(8 * i, 8 * i + 8, read_latent, acc)

    def nothing():
        pass

    for k in range(4):
        act, res, out = (act_a, None, act_b) if k % 2 == 0 else (act_b, act_a, act_a)
        halos = halo_messages(k, act)
        for h in halos:
            h.start()
        if k == 0:
            def first_wait():
                w_stage2(0)
                w_stage1(1)

            def second_wait():
                w_swap(0)
                w_stage2(1)
                w_arrived(0)
                relayout(0)
        else:
            def first_wait(k=k):
                w_arrived(k)
                w_stage2(k + 1)

            def second_wait(k=k):
                relayout(k)
        vec = all_sum(k, acc, (first_wait, second_wait))
        sc, mv = scales(k, vec)
        for h in halos:
            h.wait()
        w_swap(k + 1)
        if k < 3:
            w_stage1(k + 2)
        normalize(k, act, sc, mv)
        acc = convolve(k, res, out)

    halos = halo_messages(4, act_a)
    for h in halos:
        h.start()
    feat_copy = pltpu.make_async_copy(fbuf, feat_hbm, sem_out.at[0])
    feat_copy.start()
    w_arrived(4)
    relayout(4)
    for h in halos:
        h.wait()
    for t in range(3):
        act_a[0, :, 128 * t : 128 * t + 128] = (act_a[0, :, 128 * t : 128 * t + 128].astype(f32) * top).astype(bf16)
        es[0, t] = hc[4, 0, t] * (edge_rows * west)
    edges_to_matrix(TH // 2, 2, 1)

    def tails4(p, carry):
        pair = act_a[2 * p, :, 256:384].astype(f32) + pltpu.roll(act_a[2 * p + 1, :, 256:384].astype(f32), 64, 1)
        r0[p, :, :] = pair.astype(bf16)
        return carry

    lax.fori_loop(0, TH // 2, tails4, 0)
    edge_dot(4, TH // 2)
    half = TH // 2

    def every_other(first, lanes):
        return jnp.concatenate([act_a[2 * p + first, :, lanes] for p in range(half)], axis=0)

    parts = [every_other(a, slice(0, 256)) for a in range(3)]
    parts.append(r0[0:half].reshape(half * TW, 128))
    parts.append(every_other(2, slice(256, 384)))
    block_dot(4, parts)
    extra4 = split(bias_ref[4:5, :])

    def last(p, carry):
        place_edges(p, p, half, False)
        tiles = [o + extra4[t] for t, o in enumerate(taps_sum(p, TW // 2, 2))]
        rbuf[p] = jnp.concatenate([tiles[0], tiles[1], tiles[2][:, 0:64]], axis=1).astype(bf16)
        return carry

    lax.fori_loop(0, half, last, 0)
    red_copy = pltpu.make_async_copy(rbuf, red_hbm, sem_out.at[1])
    red_copy.start()
    for ref, sem in pending_sends:
        pltpu.make_async_copy(ref, ref, sem).wait()
    feat_copy.wait()
    red_copy.wait()


def local(latent, conv_weights, conv_bias, norm_gain, norm_shift, time_shift):
    vmem, anywhere = pl.BlockSpec(memory_space=pltpu.VMEM), pl.BlockSpec(memory_space=pl.ANY)
    return pl.pallas_call(
        kernel,
        out_shape=(
            jax.ShapeDtypeStruct((TH, TW, C), bf16),
            jax.ShapeDtypeStruct((TH // 2, TW // 2, C), bf16),
        ),
        in_specs=[anywhere, anywhere, vmem, vmem, vmem, vmem],
        out_specs=(anywhere, anywhere),
        scratch_shapes=[
            pltpu.VMEM((TH, TW, C), bf16),
            pltpu.VMEM((5, SHARD, C), bf16),
            pltpu.VMEM((TH + 2, TW, 384), bf16),
            pltpu.VMEM((TH + 2, TW, 384), bf16),
            pltpu.VMEM((TH + 2, TW, 384), bf16),
            pltpu.VMEM((TH + 2, TW, 128), bf16),
            pltpu.VMEM((2 * TH, 1024), bf16),
            pltpu.VMEM((8, RB, 80, 128), f32),
            pltpu.VMEM((8, 2 * TH, 128), f32),
            pltpu.VMEM((5, 2, 3, 48, 128), f32),
            pltpu.VMEM((2, 3, 48, 128), f32),
            pltpu.VMEM((5, 2, 3, TH, 128), f32),
            pltpu.VMEM((5, 2, NR, 240, 128), bf16),
            pltpu.VMEM((2, 1024, 1024), bf16),
            pltpu.VMEM((384, 384), bf16),
            pltpu.VMEM((4, 2, 8, 128), f32),
            pltpu.VMEM((4, NCOL - 1, 8, 128), f32),
            pltpu.VMEM((4, NR - 1, 8, 128), f32),
            pltpu.VMEM((TH, TW, C), bf16),
            pltpu.VMEM((TH // 2, TW // 2, C), bf16),
            pltpu.SemaphoreType.DMA((5,)),
            pltpu.SemaphoreType.DMA((2,)),
            pltpu.SemaphoreType.DMA((5, 3)),
            pltpu.SemaphoreType.DMA((5, 3)),
            pltpu.SemaphoreType.DMA((5, 8)),
            pltpu.SemaphoreType.DMA((5, 8)),
            pltpu.SemaphoreType.DMA((4, 2)),
            pltpu.SemaphoreType.DMA((4, 2)),
        ],
        compiler_params=pltpu.CompilerParams(
            collective_id=0, has_side_effects=True, vmem_limit_bytes=60 * 1024 * 1024
        ),
        name="down_block",
    )(latent, conv_weights, conv_bias, norm_gain, norm_shift, time_shift)


def solution(mesh):
    split = Mesh(mesh.devices.reshape(NY, NX, NZ, NC), ("rows_0", "rows_1", "cols_0", "cols_1"))
    placed = (P(ROWS, COLS, None), P(None, ROWS, None), P(), P(), P(), P())
    return jax.shard_map(
        local,
        mesh=split,
        in_specs=placed,
        out_specs=(P(ROWS, COLS, None), P(ROWS, COLS, None)),
        check_vma=False,
    )
```

```python
import functools
import itertools

import jax
import jax.numpy as jnp
from jax import lax
from jax.experimental import pallas as pl
from jax.experimental.pallas import tpu as pltpu
from jax.sharding import Mesh
from jax.sharding import PartitionSpec as P

f32, bf16 = jnp.float32, jnp.bfloat16
MESH = pl.DeviceIdType.MESH
ROWS = ("rows_0", "rows_1")
COLS = ("cols_0", "cols_1")
NY, NX, NZ, NC = 4, 4, 4, 2
NR, NCOL = NY * NX, NZ * NC
C = 320
TH, TW = 32, 64
SHARD = 180
RB = 16
EPS = 1e-05


def padded(row, width=384):
    return jnp.concatenate([row, jnp.zeros((row.shape[0], width - row.shape[1]), row.dtype)], axis=1)


def window_tiles():
    tiles = []
    for tile in range(9 * C // 16):
        holders = []
        for r in range(NR):
            first = SHARD * r // 16
            last = (SHARD * (r + 1) - 1) // 16
            if first <= tile <= last:
                holders.append((r, tile - first))
        tiles.append(holders)
    return tiles


WINDOWS = window_tiles()


def others():
    sizes = (NY, NX, NZ, NC)
    steps = [o for o in itertools.product(*[range(n) for n in sizes]) if any(o)]
    return sorted(steps, key=lambda o: -sum(2 * min(v, n - v) for v, n in zip(o[:3], sizes)) - o[3])


OTHERS = others()


def kernel(
    lat_hbm, w_hbm, bias_ref, gain_ref, shift_ref, time_ref,
    feat_hbm, red_hbm,
    lat, wl, act_a, act_b, xs, r0, edge_mat, zs, ze, hc, es, cs, gath, wk, to_group, to_channel,
    ar_src, ar_got, fbuf, rbuf,
    sem_in, sem_out, ws_send, ws_recv, halo_send, halo_recv, ar_send, ar_recv, everyone,
):
    y, x = lax.axis_index("rows_0"), lax.axis_index("rows_1")
    z, core = lax.axis_index("cols_0"), lax.axis_index("cols_1")
    r, c = y * NX + x, z * NC + core

    def dev(rr, cc):
        return (rr // NX, lax.rem(rr, NX), cc // NC, lax.rem(cc, NC))

    def row_peer(j):
        return dev(lax.rem(r + j, NR), c)

    def col_peer(j):
        return dev(r, lax.rem(c + j, NCOL))

    up, down = lax.rem(r + NR - 1, NR), lax.rem(r + 1, NR)
    left, right = lax.rem(c + NCOL - 1, NCOL), lax.rem(c + 1, NCOL)

    lat_copies = []
    for i in range(4):
        cp = pltpu.make_async_copy(lat_hbm.at[pl.ds(8 * i, 8)], lat.at[pl.ds(8 * i, 8)], sem_in.at[i])
        cp.start()
        lat_copies.append(cp)
    w_copy = pltpu.make_async_copy(w_hbm, wl, sem_in.at[4])
    w_copy.start()

    barrier = pltpu.get_barrier_semaphore()
    peers = [row_peer(j) for j in range(1, NR)] + [col_peer(j) for j in range(1, NCOL)]
    for peer in peers:
        pl.semaphore_signal(barrier, inc=1, device_id=peer, device_id_type=MESH)

    major = jnp.where(core == 0, y, x)
    minor = jnp.where(core == 0, x, y)
    slot = 4 * major + minor
    w_copy.wait()
    off = lax.rem(4 * r, 16)
    row_id = lax.broadcasted_iota(jnp.int32, (96, SHARD), 0) + 96 * core
    col_id = lax.broadcasted_iota(jnp.int32, (96, SHARD), 1) + off
    place = jnp.where(row_id == col_id, 1.0, 0.0).astype(bf16)

    def prepare(k):
        half = jnp.dot(place, wl[k], preferred_element_type=f32)
        gath[k, core, slot, 0:96] = half[:, 0:128].astype(bf16)
        gath[k, core, slot, 96:192] = half[:, 128:256].astype(bf16)
        tail = jnp.concatenate([half[0:48, 256:320], half[48:96, 256:320]], axis=1)
        gath[k, core, slot, 192:240] = tail.astype(bf16)

    prepare(0)
    ci = lax.broadcasted_iota(jnp.int32, (384, 128), 0)
    gi = lax.broadcasted_iota(jnp.int32, (384, 128), 1)
    to_group[...] = jnp.where(((ci * 6554) >> 16) == gi, 1.0, 0.0).astype(bf16)
    ci = lax.broadcasted_iota(jnp.int32, (128, 384), 1)
    gi = lax.broadcasted_iota(jnp.int32, (128, 384), 0)
    to_channel[...] = jnp.where(((ci * 6554) >> 16) == gi, 1.0, 0.0).astype(bf16)

    pl.semaphore_wait(barrier, len(peers))
    for j in range(1, NR):
        pl.semaphore_signal(everyone, inc=1, device_id=row_peer(j), device_id_type=MESH)

    def along(step_minor, step_major):
        mi = lax.rem(minor + step_minor, 4)
        ma = lax.rem(major + step_major, 4)
        return (jnp.where(core == 0, ma, mi), jnp.where(core == 0, mi, ma), z, core)

    pending_sends = []

    def w_stage1(k):
        mine = gath.at[k, core, slot]
        for j in range(1, 4):
            pltpu.make_async_remote_copy(mine, mine, ws_send.at[k, 0], ws_recv.at[k, 0], along(j, 0), MESH).start()
        pending_sends.append((gath.at[k, 0, 0:3], ws_send.at[k, 0]))

    def w_stage2(k):
        three = gath.at[k, 0, 0:3]
        pltpu.make_async_copy(three, three, ws_recv.at[k, 0]).wait()
        mine = gath.at[k, core, pl.ds(4 * major, 4)]
        for j in range(1, 4):
            pltpu.make_async_remote_copy(mine, mine, ws_send.at[k, 1], ws_recv.at[k, 1], along(0, j), MESH).start()
        pending_sends.append((gath.at[k, 0, 0:12], ws_send.at[k, 1]))

    def w_swap(k):
        twelve = gath.at[k, 0, 0:12]
        pltpu.make_async_copy(twelve, twelve, ws_recv.at[k, 1]).wait()
        mine = gath.at[k, core]
        pltpu.make_async_remote_copy(
            mine, mine, ws_send.at[k, 2], ws_recv.at[k, 2], (y, x, z, 1 - core), MESH
        ).start()
        pending_sends.append((gath.at[k, 0], ws_send.at[k, 2]))

    def w_arrived(k):
        every = gath.at[k, 0]
        pltpu.make_async_copy(every, every, ws_recv.at[k, 2]).wait()

    w_stage1(0)

    lane = lax.broadcasted_iota(jnp.int32, (1, 128), 1)
    low = lane < 64

    def relayout(k):
        wbuf = wk.at[k % 2]

        def piece(holder, part):
            rr, l = holder
            h, l6 = l // 6, l % 6
            s = rr if h == 0 else (rr % NX) * NY + rr // NX
            if part < 2:
                return gath[k, h, s, 96 * part + 16 * l6 : 96 * part + 16 * l6 + 16]
            t = gath[k, h, s, 192 + 16 * (l6 % 3) : 208 + 16 * (l6 % 3)].astype(f32)
            return t if l6 < 3 else pltpu.roll(t, 64, 1)

        def tile(t, part):
            return functools.reduce(lambda p, q: p + q, [piece(h, part) for h in WINDOWS[t]])

        for a in range(3):
            for u in range(20):
                row = 256 * a + 16 * u if u < 16 else 768 + 64 * a + 16 * (u - 16)
                tails = []
                for b in range(3):
                    t = 20 * (3 * a + b) + u
                    for part in range(2):
                        wbuf[row : row + 16, 256 * b + 128 * part : 256 * b + 128 * part + 128] = tile(t, part)
                    tails.append(jnp.where(low, tile(t, 2), 0.0))
                wbuf[row : row + 16, 768:896] = (tails[0] + pltpu.roll(tails[1], 64, 1)).astype(bf16)
                wbuf[row : row + 16, 896:1024] = tails[2].astype(bf16)

    zero_acc = tuple(jnp.zeros((8, 128), f32) for _ in range(6))

    def fold(v):
        return jnp.sum(v.reshape(v.shape[0] // 8, 8, 128), axis=0)

    def add_stats(acc, tiles):
        sums = [acc[t] + fold(tiles[t]) for t in range(3)]
        squares = [acc[3 + t] + fold(tiles[t] * tiles[t]) for t in range(3)]
        return tuple(sums + squares)

    def stage_cols(phase, row, tiles):
        for t in range(3):
            cs[phase, 0, t, pl.ds(row, 1), :] = tiles[t][0:1]
            cs[phase, 1, t, pl.ds(row, 1), :] = tiles[t][63:64]

    def halo_messages(phase, act):
        msgs = [
            (act.at[TH], act.at[0], dev(down, c)),
            (cs.at[phase, 1], hc.at[phase, 0, :, 8:40, :], dev(r, right)),
            (cs.at[phase, 1, :, 24:32, :], hc.at[phase, 0, :, 0:8, :], dev(down, right)),
        ]
        if phase < 4:
            msgs += [
                (act.at[1], act.at[TH + 1], dev(up, c)),
                (cs.at[phase, 0], hc.at[phase, 1, :, 8:40, :], dev(r, left)),
                (cs.at[phase, 0, :, 24:32, :], hc.at[phase, 1, :, 0:8, :], dev(down, left)),
                (cs.at[phase, 1, :, 0:8, :], hc.at[phase, 0, :, 40:48, :], dev(up, right)),
                (cs.at[phase, 0, :, 0:8, :], hc.at[phase, 1, :, 40:48, :], dev(up, left)),
            ]
        return [
            pltpu.make_async_remote_copy(s, d, halo_send.at[phase, i], halo_recv.at[phase, i], to, MESH)
            for i, (s, d, to) in enumerate(msgs)
        ]

    def thirds(v):
        hi = v.astype(bf16).astype(f32)
        mid = (v - hi).astype(bf16).astype(f32)
        return jnp.concatenate([hi, mid, v - hi - mid], axis=0).astype(bf16)

    def send_sums(phase, acc):
        sums = jnp.concatenate(
            [jnp.concatenate(acc[0:3], axis=1), jnp.concatenate(acc[3:6], axis=1)], axis=0
        )
        got = jnp.dot(thirds(sums), to_group[...], preferred_element_type=f32)
        got = got[0:16] + got[16:32] + got[32:48]
        own = jnp.sum(got[0:8], axis=0, keepdims=True) + pltpu.roll(jnp.sum(got[8:16], axis=0, keepdims=True), 32, 1)
        ar_src[phase] = own
        me = (y, x, z, core)
        for j, offset in enumerate(OTHERS):
            to = tuple(lax.rem(m + o, n) if o else m for m, o, n in zip(me, offset, (NY, NX, NZ, NC)))
            pltpu.make_async_remote_copy(
                ar_src.at[phase], ar_got.at[phase, j], ar_send.at[phase], ar_recv.at[phase], to, MESH
            ).start()
        pending_sends.append((ar_got.at[phase], ar_send.at[phase]))
        return own

    def all_sums(phase, own):
        every = ar_got.at[phase]
        pltpu.make_async_copy(every, every, ar_recv.at[phase]).wait()
        return own + jnp.sum(ar_got[phase], axis=0)

    def scales(phase, vec):
        count = float(TH * NR * TW * NCOL * (C // 32))
        mean = vec / count
        spread = jnp.maximum(pltpu.roll(mean, 96, 1) - mean * mean, 0.0)
        scale = lax.rsqrt(spread + EPS)
        pair = jnp.concatenate([scale, mean * scale], axis=0)
        pair = jnp.where(lane < 32, pair, 0.0)
        tot = jnp.dot(thirds(jnp.concatenate([pair, jnp.zeros((6, 128), f32)], axis=0)), to_channel[...], preferred_element_type=f32)
        tot = tot[0:8] + tot[8:16] + tot[16:24]
        gain = padded(0.5 * gain_ref[phase : phase + 1, :])
        scale = tot[0:1] * gain
        move = padded(0.5 * shift_ref[phase : phase + 1, :]) - tot[1:2] * gain
        return [scale[:, 128 * t : 128 * t + 128] for t in range(3)], [move[:, 128 * t : 128 * t + 128] for t in range(3)]

    def silu_of(v, scale, move):
        half = v * scale + move
        return half + half * jnp.tanh(half)

    def on(cond):
        return jnp.where(cond, 1.0, 0.0).astype(f32)

    top, bottom = on(r > 0), on(r < NR - 1)
    west, east = on(c > 0), on(c < NCOL - 1)

    def edges_to_matrix(rows, stride, sides):
        for side in range(sides):
            at = slice(rows * side, rows * side + rows)
            taps = [
                [es[side, t, pl.ds(7 + a, rows, stride=stride) if stride > 1 else pl.ds(7 + a, rows), :] for t in range(3)]
                for a in range(3)
            ]
            for a in range(3):
                for t in range(2):
                    edge_mat[at, 256 * a + 128 * t : 256 * a + 128 * t + 128] = taps[a][t].astype(bf16)
            edge_mat[at, 768:896] = (taps[0][2] + pltpu.roll(taps[1][2], 64, 1)).astype(bf16)
            edge_mat[at, 896:1024] = taps[2][2].astype(bf16)

    er = lax.broadcasted_iota(jnp.int32, (48, 1), 0)
    edge_rows = jnp.where(er < 8, top, jnp.where(er < 40, 1.0, bottom))

    def normalize(phase, act, sc, mv, between):
        def one(i, prev):
            m = jnp.where(i == 0, top, jnp.where(i == TH + 1, bottom, 1.0))
            tiles = []
            for t in range(3):
                v = act[i, :, 128 * t : 128 * t + 128].astype(f32)
                tiles.append(silu_of(v, sc[t] * m, mv[t] * m))
                xs[i, :, 128 * t : 128 * t + 128] = tiles[t].astype(bf16)
            r0[i, :, :] = (prev + pltpu.roll(tiles[2], 64, 1)).astype(bf16)
            return tiles[2]

        prev = lax.fori_loop(0, TH // 2, one, jnp.zeros((TW, 128), f32))
        between()
        lax.fori_loop(TH // 2, TH + 2, one, prev)
        for side, mask in ((0, west), (1, east)):
            for t in range(3):
                es[side, t] = silu_of(hc[phase, side, t], sc[t], mv[t]) * (edge_rows * mask)
        edges_to_matrix(TH, 1, 2)

    def edge_dot(k, rows):
        for n in range(4):
            o = jnp.dot(edge_mat[0:rows], wk[k % 2, :, 256 * n : 256 * n + 256], preferred_element_type=f32)
            ze[2 * n, 0:rows] = o[:, 0:128]
            ze[2 * n + 1, 0:rows] = o[:, 128:256]

    def block_dot(k, parts):
        lhs = jnp.concatenate(parts, axis=1)
        for n in range(4):
            o = jnp.dot(lhs, wk[k % 2, :, 256 * n : 256 * n + 256], preferred_element_type=f32)
            zs[2 * n, :, 8 : 8 + TW, :] = o[:, 0:128].reshape(RB, TW, 128)
            zs[2 * n + 1, :, 8 : 8 + TW, :] = o[:, 128:256].reshape(RB, TW, 128)

    def taps_sum(rr, width, stride):
        def at(t, first):
            if stride > 1:
                return zs[t, rr, pl.ds(first, width, stride=stride), :]
            return zs[t, rr, first : first + width, :]

        outs = [at(t, 7) + at(2 + t, 8) + at(4 + t, 9) for t in range(2)]
        tail = at(6, 7) + pltpu.roll(at(6, 8), 64, 1) + at(7, 9)
        return outs + [jnp.where(low, tail, 0.0)]

    def place_edges(rr, row, rows, both):
        for t in (0, 1, 6):
            zs[t, rr, 7:8, :] = ze[t, pl.ds(row, 1), :]
        if both:
            for t in (4, 5, 7):
                zs[t, rr, 72:73, :] = ze[t, pl.ds(rows + row, 1), :]

    def split(row):
        row = padded(row)
        return [row[:, 128 * t : 128 * t + 128] for t in range(3)]

    def convolve(k, res, out):
        extra = split(bias_ref[k : k + 1, :] + (time_ref[k // 2 : k // 2 + 1, :] if k % 2 == 0 else 0.0))
        edge_dot(k, 2 * TH)

        def block(i, acc):
            first = i * RB
            parts = [xs[pl.ds(first + a, RB), :, 0:256].reshape(RB * TW, 256) for a in range(3)]
            parts.append(r0[pl.ds(first + 1, RB)].reshape(RB * TW, 128))
            parts.append(xs[pl.ds(first + 2, RB), :, 256:384].reshape(RB * TW, 128))
            block_dot(k, parts)

            def one(rr, acc):
                row = first + rr
                place_edges(rr, row, TH, True)
                tiles = []
                for t, o in enumerate(taps_sum(rr, TW, 1)):
                    o = o + extra[t]
                    if res is not None:
                        o = o + res[row + 1, :, 128 * t : 128 * t + 128].astype(f32)
                    o = o.astype(bf16)
                    out[row + 1, :, 128 * t : 128 * t + 128] = o
                    tiles.append(o.astype(f32))
                stage_cols(k + 1, row, tiles)
                if k == 3:
                    fbuf[row] = jnp.concatenate([tiles[0], tiles[1], tiles[2][:, 0:64]], axis=1).astype(bf16)
                    return acc
                return add_stats(acc, tiles)

            return lax.fori_loop(0, RB, one, acc)

        return lax.fori_loop(0, TH // RB, block, zero_acc)

    def read_latent(i, acc):
        v = lat[i].astype(f32)
        tiles = [v[:, 0:128], v[:, 128:256], padded(v[:, 256:320], 128)]
        for t in range(3):
            act_a[i + 1, :, 128 * t : 128 * t + 128] = tiles[t].astype(bf16)
        stage_cols(0, i, tiles)
        return add_stats(acc, tiles)

    acc = zero_acc
    for i in range(4):
        lat_copies[i].wait()
        acc = lax.fori_loop(8 * i, 8 * i + 8, read_latent, acc)

    pl.semaphore_wait(everyone, NR - 1)

    def nothing():
        pass

    for k in range(4):
        act, res, out = (act_a, None, act_b) if k % 2 == 0 else (act_b, act_a, act_a)
        own = send_sums(k, acc)
        halos = halo_messages(k, act)
        for h in halos:
            h.start()
        if k == 0:
            for later in range(1, 5):
                prepare(later)
            for i in range(2):
                wk[i, 960:1024, :] = jnp.zeros((64, 1024), bf16)
            w_stage2(0)
        else:
            w_arrived(k)
            relayout(k)
        w_stage1(k + 1)
        for h in halos:
            h.wait()
        sc, mv = scales(k, all_sums(k, own))
        normalize(k, act, sc, mv, functools.partial(w_swap, 0) if k == 0 else nothing)
        if k == 0:
            w_arrived(0)
            relayout(0)
        w_stage2(k + 1)
        acc = convolve(k, res, out)
        w_swap(k + 1)

    halos = halo_messages(4, act_a)
    for h in halos:
        h.start()
    feat_copy = pltpu.make_async_copy(fbuf, feat_hbm, sem_out.at[0])
    feat_copy.start()
    w_arrived(4)
    relayout(4)
    for h in halos:
        h.wait()
    for t in range(3):
        act_a[0, :, 128 * t : 128 * t + 128] = (act_a[0, :, 128 * t : 128 * t + 128].astype(f32) * top).astype(bf16)
        es[0, t] = hc[4, 0, t] * (edge_rows * west)
    edges_to_matrix(TH // 2, 2, 1)

    def tails4(p, carry):
        pair = act_a[2 * p, :, 256:384].astype(f32) + pltpu.roll(act_a[2 * p + 1, :, 256:384].astype(f32), 64, 1)
        r0[p, :, :] = pair.astype(bf16)
        return carry

    lax.fori_loop(0, TH // 2, tails4, 0)
    edge_dot(4, TH // 2)
    half = TH // 2

    def every_other(first, lanes):
        return jnp.concatenate([act_a[2 * p + first, :, lanes] for p in range(half)], axis=0)

    parts = [every_other(a, slice(0, 256)) for a in range(3)]
    parts.append(r0[0:half].reshape(half * TW, 128))
    parts.append(every_other(2, slice(256, 384)))
    block_dot(4, parts)
    extra4 = split(bias_ref[4:5, :])

    def last(p, carry):
        place_edges(p, p, half, False)
        tiles = [o + extra4[t] for t, o in enumerate(taps_sum(p, TW // 2, 2))]
        rbuf[p] = jnp.concatenate([tiles[0], tiles[1], tiles[2][:, 0:64]], axis=1).astype(bf16)
        return carry

    lax.fori_loop(0, half, last, 0)
    red_copy = pltpu.make_async_copy(rbuf, red_hbm, sem_out.at[1])
    red_copy.start()
    for ref, sem in pending_sends:
        pltpu.make_async_copy(ref, ref, sem).wait()
    feat_copy.wait()
    red_copy.wait()


def local(latent, conv_weights, conv_bias, norm_gain, norm_shift, time_shift):
    vmem, anywhere = pl.BlockSpec(memory_space=pltpu.VMEM), pl.BlockSpec(memory_space=pl.ANY)
    return pl.pallas_call(
        kernel,
        out_shape=(
            jax.ShapeDtypeStruct((TH, TW, C), bf16),
            jax.ShapeDtypeStruct((TH // 2, TW // 2, C), bf16),
        ),
        in_specs=[anywhere, anywhere, vmem, vmem, vmem, vmem],
        out_specs=(anywhere, anywhere),
        scratch_shapes=[
            pltpu.VMEM((TH, TW, C), bf16),
            pltpu.VMEM((5, SHARD, C), bf16),
            pltpu.VMEM((TH + 2, TW, 384), bf16),
            pltpu.VMEM((TH + 2, TW, 384), bf16),
            pltpu.VMEM((TH + 2, TW, 384), bf16),
            pltpu.VMEM((TH + 2, TW, 128), bf16),
            pltpu.VMEM((2 * TH, 1024), bf16),
            pltpu.VMEM((8, RB, 80, 128), f32),
            pltpu.VMEM((8, 2 * TH, 128), f32),
            pltpu.VMEM((5, 2, 3, 48, 128), f32),
            pltpu.VMEM((2, 3, 48, 128), f32),
            pltpu.VMEM((5, 2, 3, TH, 128), f32),
            pltpu.VMEM((5, 2, NR, 240, 128), bf16),
            pltpu.VMEM((2, 1024, 1024), bf16),
            pltpu.VMEM((384, 128), bf16),
            pltpu.VMEM((128, 384), bf16),
            pltpu.VMEM((4, 1, 128), f32),
            pltpu.VMEM((4, NR * NCOL - 1, 1, 128), f32),
            pltpu.VMEM((TH, TW, C), bf16),
            pltpu.VMEM((TH // 2, TW // 2, C), bf16),
            pltpu.SemaphoreType.DMA((5,)),
            pltpu.SemaphoreType.DMA((2,)),
            pltpu.SemaphoreType.DMA((5, 3)),
            pltpu.SemaphoreType.DMA((5, 3)),
            pltpu.SemaphoreType.DMA((5, 8)),
            pltpu.SemaphoreType.DMA((5, 8)),
            pltpu.SemaphoreType.DMA((4,)),
            pltpu.SemaphoreType.DMA((4,)),
            pltpu.SemaphoreType.REGULAR,
        ],
        compiler_params=pltpu.CompilerParams(
            collective_id=0, has_side_effects=True, vmem_limit_bytes=60 * 1024 * 1024
        ),
        name="down_block",
    )(latent, conv_weights, conv_bias, norm_gain, norm_shift, time_shift)


def solution(mesh):
    split = Mesh(mesh.devices.reshape(NY, NX, NZ, NC), ("rows_0", "rows_1", "cols_0", "cols_1"))
    placed = (P(ROWS, COLS, None), P(None, ROWS, None), P(), P(), P(), P())
    return jax.shard_map(
        local,
        mesh=split,
        in_specs=placed,
        out_specs=(P(ROWS, COLS, None), P(ROWS, COLS, None)),
        check_vma=False,
    )
```

```python
import functools
import itertools

import jax
import jax.numpy as jnp
from jax import lax
from jax.experimental import pallas as pl
from jax.experimental.pallas import tpu as pltpu
from jax.sharding import Mesh
from jax.sharding import PartitionSpec as P

f32, bf16 = jnp.float32, jnp.bfloat16
MESH = pl.DeviceIdType.MESH
ROWS = ("rows_0", "rows_1")
COLS = ("cols_0", "cols_1")
NY, NX, NZ, NC = 4, 4, 4, 2
NR, NCOL = NY * NX, NZ * NC
C = 320
TH, TW = 32, 64
SHARD = 180
RB = 8
NB = TH // RB
EPS = 1e-05


def padded(row, width=384):
    return jnp.concatenate([row, jnp.zeros((row.shape[0], width - row.shape[1]), row.dtype)], axis=1)


def window_tiles():
    tiles = []
    for tile in range(9 * C // 16):
        holders = []
        for r in range(NR):
            first = SHARD * r // 16
            last = (SHARD * (r + 1) - 1) // 16
            if first <= tile <= last:
                holders.append((r, tile - first))
        tiles.append(holders)
    return tiles


WINDOWS = window_tiles()


def others():
    sizes = (NY, NX, NZ, NC)
    steps = [o for o in itertools.product(*[range(n) for n in sizes]) if any(o)]
    return sorted(steps, key=lambda o: -sum(2 * min(v, n - v) for v, n in zip(o[:3], sizes)) - o[3])


OTHERS = others()


def kernel(
    lat_hbm, w_hbm, bias_ref, gain_ref, shift_ref, time_ref,
    feat_hbm, red_hbm,
    lat, wl, act_a, act_b, xs, r0, edge_mat, zs_even, zs_odd, hc, es, cs, gath, wk, to_group, to_channel,
    ar_src, ar_got, ar_first, fbuf, rbuf,
    sem_in, sem_out, ws_send, ws_recv, halo_send, halo_recv, ar_send, ar_recv,
):
    y, x = lax.axis_index("rows_0"), lax.axis_index("rows_1")
    z, core = lax.axis_index("cols_0"), lax.axis_index("cols_1")
    r, c = y * NX + x, z * NC + core

    def dev(rr, cc):
        return (rr // NX, lax.rem(rr, NX), cc // NC, lax.rem(cc, NC))

    def row_peer(j):
        return dev(lax.rem(r + j, NR), c)

    def col_peer(j):
        return dev(r, lax.rem(c + j, NCOL))

    up, down = lax.rem(r + NR - 1, NR), lax.rem(r + 1, NR)
    left, right = lax.rem(c + NCOL - 1, NCOL), lax.rem(c + 1, NCOL)

    lat_copies = []
    for i in range(4):
        cp = pltpu.make_async_copy(lat_hbm.at[pl.ds(8 * i, 8)], lat.at[pl.ds(8 * i, 8)], sem_in.at[i])
        cp.start()
        lat_copies.append(cp)
    w_copy = pltpu.make_async_copy(w_hbm, wl, sem_in.at[4])
    w_copy.start()

    barrier = pltpu.get_barrier_semaphore()
    peers = [row_peer(j) for j in range(1, NR)] + [col_peer(j) for j in range(1, NCOL)]
    for peer in peers:
        pl.semaphore_signal(barrier, inc=1, device_id=peer, device_id_type=MESH)

    major = jnp.where(core == 0, y, x)
    minor = jnp.where(core == 0, x, y)
    slot = 4 * major + minor
    w_copy.wait()
    off = lax.rem(4 * r, 16)
    row_id = lax.broadcasted_iota(jnp.int32, (96, SHARD), 0) + 96 * core
    col_id = lax.broadcasted_iota(jnp.int32, (96, SHARD), 1) + off
    place = jnp.where(row_id == col_id, 1.0, 0.0).astype(bf16)

    def prepare(k):
        half = jnp.dot(place, wl[k], preferred_element_type=f32)
        gath[k, core, slot, 0:96] = half[:, 0:128].astype(bf16)
        gath[k, core, slot, 96:192] = half[:, 128:256].astype(bf16)
        tail = jnp.concatenate([half[0:48, 256:320], half[48:96, 256:320]], axis=1)
        gath[k, core, slot, 192:240] = tail.astype(bf16)

    prepare(0)
    ci = lax.broadcasted_iota(jnp.int32, (384, 128), 0)
    gi = lax.broadcasted_iota(jnp.int32, (384, 128), 1)
    to_group[...] = jnp.where(((ci * 6554) >> 16) == gi, 1.0, 0.0).astype(bf16)
    ci = lax.broadcasted_iota(jnp.int32, (128, 384), 1)
    gi = lax.broadcasted_iota(jnp.int32, (128, 384), 0)
    to_channel[...] = jnp.where(((ci * 6554) >> 16) == gi, 1.0, 0.0).astype(bf16)

    pl.semaphore_wait(barrier, len(peers))

    def along(step_minor, step_major):
        mi = lax.rem(minor + step_minor, 4)
        ma = lax.rem(major + step_major, 4)
        return (jnp.where(core == 0, ma, mi), jnp.where(core == 0, mi, ma), z, core)

    pending_sends = []

    def w_stage1(k):
        mine = gath.at[k, core, slot]
        for j in range(1, 4):
            pltpu.make_async_remote_copy(mine, mine, ws_send.at[k, 0], ws_recv.at[k, 0], along(j, 0), MESH).start()
        pending_sends.append((gath.at[k, 0, 0:3], ws_send.at[k, 0]))

    def w_stage2(k):
        three = gath.at[k, 0, 0:3]
        pltpu.make_async_copy(three, three, ws_recv.at[k, 0]).wait()
        mine = gath.at[k, core, pl.ds(4 * major, 4)]
        for j in range(1, 4):
            pltpu.make_async_remote_copy(mine, mine, ws_send.at[k, 1], ws_recv.at[k, 1], along(0, j), MESH).start()
        pending_sends.append((gath.at[k, 0, 0:12], ws_send.at[k, 1]))

    def w_swap(k):
        twelve = gath.at[k, 0, 0:12]
        pltpu.make_async_copy(twelve, twelve, ws_recv.at[k, 1]).wait()
        mine = gath.at[k, core]
        pltpu.make_async_remote_copy(
            mine, mine, ws_send.at[k, 2], ws_recv.at[k, 2], (y, x, z, 1 - core), MESH
        ).start()
        pending_sends.append((gath.at[k, 0], ws_send.at[k, 2]))

    def w_arrived(k):
        every = gath.at[k, 0]
        pltpu.make_async_copy(every, every, ws_recv.at[k, 2]).wait()


    lane = lax.broadcasted_iota(jnp.int32, (1, 128), 1)
    low = lane < 64

    def relayout(k):
        wbuf = wk.at[k % 2]

        def piece(holder, part):
            rr, l = holder
            h, l6 = l // 6, l % 6
            s = rr if h == 0 else (rr % NX) * NY + rr // NX
            if part < 2:
                return gath[k, h, s, 96 * part + 16 * l6 : 96 * part + 16 * l6 + 16]
            t = gath[k, h, s, 192 + 16 * (l6 % 3) : 208 + 16 * (l6 % 3)].astype(f32)
            return t if l6 < 3 else pltpu.roll(t, 64, 1)

        def tile(t, part):
            return functools.reduce(lambda p, q: p + q, [piece(h, part) for h in WINDOWS[t]])

        for a in range(3):
            for u in range(20):
                row = 256 * a + 16 * u if u < 16 else 768 + 64 * a + 16 * (u - 16)
                tails = []
                for b in range(3):
                    t = 20 * (3 * a + b) + u
                    for part in range(2):
                        wbuf[row : row + 16, 256 * b + 128 * part : 256 * b + 128 * part + 128] = tile(t, part)
                    tails.append(jnp.where(low, tile(t, 2), 0.0))
                wbuf[row : row + 16, 768:896] = (tails[0] + pltpu.roll(tails[1], 64, 1)).astype(bf16)
                wbuf[row : row + 16, 896:1024] = tails[2].astype(bf16)

    zero_acc = tuple(jnp.zeros((8, 128), f32) for _ in range(6))

    def fold(v):
        return jnp.sum(v.reshape(v.shape[0] // 8, 8, 128), axis=0)

    def add_stats(acc, tiles):
        sums = [acc[t] + fold(tiles[t]) for t in range(3)]
        squares = [acc[3 + t] + fold(tiles[t] * tiles[t]) for t in range(3)]
        return tuple(sums + squares)

    def stage_cols(phase, row, tiles):
        for t in range(3):
            cs[phase, 0, t, pl.ds(row, 1), :] = tiles[t][0:1]
            cs[phase, 1, t, pl.ds(row, 1), :] = tiles[t][63:64]

    def halo_messages(phase, act):
        msgs = [
            (act.at[TH], act.at[0], dev(down, c)),
            (cs.at[phase, 1], hc.at[phase, 0, :, 8:40, :], dev(r, right)),
            (cs.at[phase, 1, :, 24:32, :], hc.at[phase, 0, :, 0:8, :], dev(down, right)),
        ]
        if phase < 4:
            msgs += [
                (act.at[1], act.at[TH + 1], dev(up, c)),
                (cs.at[phase, 0], hc.at[phase, 1, :, 8:40, :], dev(r, left)),
                (cs.at[phase, 0, :, 24:32, :], hc.at[phase, 1, :, 0:8, :], dev(down, left)),
                (cs.at[phase, 1, :, 0:8, :], hc.at[phase, 0, :, 40:48, :], dev(up, right)),
                (cs.at[phase, 0, :, 0:8, :], hc.at[phase, 1, :, 40:48, :], dev(up, left)),
            ]
        return [
            pltpu.make_async_remote_copy(s, d, halo_send.at[phase, i], halo_recv.at[phase, i], to, MESH)
            for i, (s, d, to) in enumerate(msgs)
        ]

    def thirds(v):
        hi = v.astype(bf16).astype(f32)
        mid = (v - hi).astype(bf16).astype(f32)
        return jnp.concatenate([hi, mid, v - hi - mid], axis=0).astype(bf16)

    def own_sums(acc):
        sums = jnp.concatenate(
            [jnp.concatenate(acc[0:3], axis=1), jnp.concatenate(acc[3:6], axis=1)], axis=0
        )
        got = jnp.dot(thirds(sums), to_group[...], preferred_element_type=f32)
        got = got[0:16] + got[16:32] + got[32:48]
        return jnp.sum(got[0:8], axis=0, keepdims=True) + pltpu.roll(jnp.sum(got[8:16], axis=0, keepdims=True), 32, 1)

    def send_sums(phase, own):
        ar_src[phase] = own
        me = (y, x, z, core)
        for j, offset in enumerate(OTHERS):
            to = tuple(lax.rem(m + o, n) if o else m for m, o, n in zip(me, offset, (NY, NX, NZ, NC)))
            pltpu.make_async_remote_copy(
                ar_src.at[phase], ar_got.at[phase, j], ar_send.at[phase], ar_recv.at[phase], to, MESH
            ).start()
        pending_sends.append((ar_got.at[phase], ar_send.at[phase]))

    def first_sums(own, between):
        at = 0
        for stage, (peer, n) in enumerate(((col_peer, NCOL), (row_peer, NR))):
            ar_src[4 + stage] = own
            got = ar_first.at[pl.ds(at, n - 1)]
            for j in range(1, n):
                pltpu.make_async_remote_copy(
                    ar_src.at[4 + stage], ar_first.at[at + j - 1], ar_send.at[4 + stage], ar_recv.at[4 + stage], peer(j), MESH
                ).start()
            pending_sends.append((got, ar_send.at[4 + stage]))
            between[stage]()
            pltpu.make_async_copy(got, got, ar_recv.at[4 + stage]).wait()
            own = own + jnp.sum(ar_first[at : at + n - 1], axis=0)
            at += n - 1
        return own

    def all_sums(phase, own):
        every = ar_got.at[phase]
        pltpu.make_async_copy(every, every, ar_recv.at[phase]).wait()
        return own + jnp.sum(ar_got[phase], axis=0)

    def scales(phase, vec):
        count = float(TH * NR * TW * NCOL * (C // 32))
        mean = vec / count
        spread = jnp.maximum(pltpu.roll(mean, 96, 1) - mean * mean, 0.0)
        scale = lax.rsqrt(spread + EPS)
        pair = jnp.concatenate([scale, mean * scale], axis=0)
        pair = jnp.where(lane < 32, pair, 0.0)
        tot = jnp.dot(thirds(jnp.concatenate([pair, jnp.zeros((6, 128), f32)], axis=0)), to_channel[...], preferred_element_type=f32)
        tot = tot[0:8] + tot[8:16] + tot[16:24]
        gain = padded(0.5 * gain_ref[phase : phase + 1, :])
        scale = tot[0:1] * gain
        move = padded(0.5 * shift_ref[phase : phase + 1, :]) - tot[1:2] * gain
        return [scale[:, 128 * t : 128 * t + 128] for t in range(3)], [move[:, 128 * t : 128 * t + 128] for t in range(3)]

    def silu_of(v, scale, move):
        half = v * scale + move
        return half + half * jnp.tanh(half)

    def on(cond):
        return jnp.where(cond, 1.0, 0.0).astype(f32)

    top, bottom = on(r > 0), on(r < NR - 1)
    west, east = on(c > 0), on(c < NCOL - 1)

    def edge_taps(side, rows, stride):
        def tap(t, a):
            if stride > 1:
                return es[side, t, pl.ds(7 + a, rows, stride=stride), :]
            return es[side, t, 7 + a : 7 + a + rows, :]

        cols = [tap(t, a) for a in range(3) for t in range(2)]
        return cols + [tap(2, 0) + pltpu.roll(tap(2, 1), 64, 1), tap(2, 2)]

    def edges_to_matrix():
        both = [edge_taps(side, TH, 1) for side in range(2)]
        for b in range(NB):
            for i in range(8):
                pair = [both[side][i][RB * b : RB * b + RB] for side in range(2)]
                edge_mat[2 * RB * b : 2 * RB * (b + 1), 128 * i : 128 * i + 128] = jnp.concatenate(pair, axis=0).astype(bf16)

    er = lax.broadcasted_iota(jnp.int32, (48, 1), 0)
    edge_rows = jnp.where(er < 8, top, jnp.where(er < 40, 1.0, bottom))

    def norm_rows(act, sc, mv, carry, rows):
        for i in reversed(rows):
            tiles = []
            for t in range(3):
                scale, move = sc[t], mv[t]
                if i in (0, TH + 1):
                    mask = top if i == 0 else bottom
                    scale, move = scale * mask, move * mask
                v = act[i, :, 128 * t : 128 * t + 128].astype(f32)
                tiles.append(silu_of(v, scale, move))
                xs[i, :, 128 * t : 128 * t + 128] = tiles[t].astype(bf16)
            if carry[0] is not None:
                r0[i + 1] = (tiles[2] + carry[0]).astype(bf16)
            carry[0] = pltpu.roll(tiles[2], 64, 1)

    def norm_edges(phase, sc, mv):
        for side, mask in ((0, west), (1, east)):
            for t in range(3):
                es[side, t] = silu_of(hc[phase, side, t], sc[t], mv[t]) * (edge_rows * mask)
        edges_to_matrix()

    def block_dot(k, zs, parts, edges, work):
        lhs = jnp.concatenate([jnp.concatenate(parts, axis=1), edges], axis=0)
        rows = RB * TW
        for n in range(4):
            o = jnp.dot(lhs, wk[k % 2, :, 256 * n : 256 * n + 256], preferred_element_type=f32)
            for t in range(2):
                p = o[:, 128 * t : 128 * t + 128]
                tile = 2 * n + t
                zs[tile, :, 8 : 8 + TW, :] = p[0:rows].reshape(RB, TW, 128)
                if tile in (0, 1, 6):
                    for rr in range(RB):
                        zs[tile, rr, 7:8, :] = p[rows + rr : rows + rr + 1]
                if tile in (4, 5, 7):
                    for rr in range(RB):
                        zs[tile, rr, 8 + TW : 9 + TW, :] = p[rows + RB + rr : rows + RB + rr + 1]
            for item in work[len(work) * n // 4 : len(work) * (n + 1) // 4]:
                item()

    def taps_sum(zs, rr, width, stride):
        def at(t, first):
            if stride > 1:
                return zs[t, rr, pl.ds(first, width, stride=stride), :]
            return zs[t, rr, first : first + width, :]

        outs = [at(t, 7) + at(2 + t, 8) + at(4 + t, 9) for t in range(2)]
        tail = at(6, 7) + pltpu.roll(at(6, 8), 64, 1) + at(7, 9)
        return outs + [jnp.where(low, tail, 0.0)]

    def split(row):
        row = padded(row)
        return [row[:, 128 * t : 128 * t + 128] for t in range(3)]

    def convolve(k, act, sc, mv, res, out, ahead):
        extra = split(bias_ref[k : k + 1, :] + (time_ref[k // 2 : k // 2 + 1, :] if k % 2 == 0 else 0.0))
        stats = [zero_acc]
        carry = [None]

        def norm_item(rows):
            return lambda: norm_rows(act, sc, mv, carry, rows)

        def needed(b):
            return range(RB * b, RB * b + RB if b < NB - 1 else TH + 2)

        def finish_row(zs, b, rr):
            row = RB * b + rr
            tiles = []
            for t, o in enumerate(taps_sum(zs, rr, TW, 1)):
                o = o + extra[t]
                if res is not None:
                    o = o + res[row + 1, :, 128 * t : 128 * t + 128].astype(f32)
                o = o.astype(bf16)
                out[row + 1, :, 128 * t : 128 * t + 128] = o
                tiles.append(o.astype(f32))
            for t in range(3):
                cs[k + 1, 0, t, row : row + 1, :] = tiles[t][0:1]
                cs[k + 1, 1, t, row : row + 1, :] = tiles[t][TW - 1 : TW]
            if k == 3:
                fbuf[row] = jnp.concatenate([tiles[0], tiles[1], tiles[2][:, 0:64]], axis=1).astype(bf16)
            else:
                stats[0] = add_stats(stats[0], tiles)

        def finish_item(zs, b, rr):
            return lambda: finish_row(zs, b, rr)

        norm_rows(act, sc, mv, carry, needed(NB - 1))
        if ahead is not None:
            ahead[0]()
            norm_rows(act, sc, mv, carry, range(0, RB * (NB - 1)))
            ahead[1]()
        before = []
        for step, b in enumerate(reversed(range(NB))):
            zs = zs_even if step % 2 == 0 else zs_odd
            parts = [xs[RB * b + a : RB * b + a + RB, :, 0:256].reshape(RB * TW, 256) for a in range(3)]
            parts.append(r0[RB * b + 1 : RB * b + 1 + RB].reshape(RB * TW, 128))
            parts.append(xs[RB * b + 2 : RB * b + 2 + RB, :, 256:384].reshape(RB * TW, 128))
            work = list(before)
            if b > 0 and ahead is None:
                norms = [norm_item(range(i, i + 1)) for i in reversed(needed(b - 1))]
                work = [w for pair in itertools.zip_longest(norms, work) for w in pair if w is not None]
            block_dot(k, zs, parts, edge_mat[2 * RB * b : 2 * RB * (b + 1)], work)
            before = [finish_item(zs, b, rr) for rr in reversed(range(RB))]
        for item in before:
            item()
        return stats[0]

    def read_latent(i, acc):
        v = lat[i].astype(f32)
        tiles = [v[:, 0:128], v[:, 128:256], padded(v[:, 256:320], 128)]
        for t in range(3):
            act_a[i + 1, :, 128 * t : 128 * t + 128] = tiles[t].astype(bf16)
        stage_cols(0, i, tiles)
        return add_stats(acc, tiles)

    acc = zero_acc
    for i in range(4):
        lat_copies[i].wait()
        acc = lax.fori_loop(8 * i, 8 * i + 8, read_latent, acc)


    w_stage1(0)

    for k in range(4):
        act, res, out = (act_a, None, act_b) if k % 2 == 0 else (act_b, act_a, act_a)
        own = own_sums(acc)
        halos = halo_messages(k, act)
        straight = [h for i, h in enumerate(halos) if i in (0, 1, 3, 4)]
        corners = [h for i, h in enumerate(halos) if i in (2, 5, 6, 7)]
        ahead = None
        if k == 0:
            def beside_first():
                for h in straight:
                    h.start()
                for later in range(1, 5):
                    prepare(later)
                for i in range(2):
                    wk[i, 960:1024, :] = jnp.zeros((64, 1024), bf16)

            def beside_second():
                for h in corners:
                    h.start()
                w_stage2(0)
                w_stage1(1)

            def got_first():
                w_arrived(0)
                w_stage2(1)
                relayout(0)

            ahead = (functools.partial(w_swap, 0), got_first)
            total = first_sums(own, (beside_first, beside_second))
        else:
            send_sums(k, own)
            for h in straight + corners:
                h.start()
            w_arrived(k)
            relayout(k)
            w_stage1(k + 1)
            total = all_sums(k, own)
        sc, mv = scales(k, total)
        for h in halos:
            h.wait()
        norm_edges(k, sc, mv)
        if k > 0:
            w_stage2(k + 1)
        acc = convolve(k, act, sc, mv, res, out, ahead)
        w_swap(k + 1)

    halos = halo_messages(4, act_a)
    for h in halos:
        h.start()
    feat_copy = pltpu.make_async_copy(fbuf, feat_hbm, sem_out.at[0])
    feat_copy.start()
    w_arrived(4)
    relayout(4)
    half = TH // 2
    extra4 = split(bias_ref[4:5, :])

    def reduced_parts(b):
        def every_other(first, lanes):
            return jnp.concatenate([act_a[2 * p + first, :, lanes] for p in range(RB * b, RB * b + RB)], axis=0)

        heads = [every_other(a, slice(0, 256)) for a in range(3)]
        pair = every_other(0, slice(256, 384)).astype(f32) + pltpu.roll(every_other(1, slice(256, 384)).astype(f32), 64, 1)
        return heads + [pair.astype(bf16), every_other(2, slice(256, 384))]

    def dot4(zs, parts, edges):
        lhs = jnp.concatenate(parts, axis=1)
        rows = RB * TW
        if edges is not None:
            lhs = jnp.concatenate([lhs, edges], axis=0)
        for n in range(4):
            o = jnp.dot(lhs, wk[0, :, 256 * n : 256 * n + 256], preferred_element_type=f32)
            for t in range(2):
                tile = 2 * n + t
                p = o[:, 128 * t : 128 * t + 128]
                zs[tile, :, 8 : 8 + TW, :] = p[0:rows].reshape(RB, TW, 128)
                if edges is not None and tile in (0, 1, 6):
                    for rr in range(half):
                        (zs_odd if rr < RB else zs_even)[tile, rr % RB, 7:8, :] = p[rows + rr : rows + rr + 1]

    dot4(zs_even, reduced_parts(1), None)
    for h in halos:
        h.wait()
    for t in range(3):
        act_a[0, :, 128 * t : 128 * t + 128] = (act_a[0, :, 128 * t : 128 * t + 128].astype(f32) * top).astype(bf16)
        es[0, t] = hc[4, 0, t] * (edge_rows * west)
    left_taps = jnp.concatenate(edge_taps(0, half, 2), axis=1).astype(bf16)
    dot4(zs_odd, reduced_parts(0), left_taps)

    def last(zs, first):
        def one(p, carry):
            tiles = [o + extra4[t] for t, o in enumerate(taps_sum(zs, p, TW // 2, 2))]
            rbuf[first + p] = jnp.concatenate([tiles[0], tiles[1], tiles[2][:, 0:64]], axis=1).astype(bf16)
            return carry

        lax.fori_loop(0, RB, one, 0)

    last(zs_even, RB)
    last(zs_odd, 0)
    red_copy = pltpu.make_async_copy(rbuf, red_hbm, sem_out.at[1])
    red_copy.start()
    for ref, sem in pending_sends:
        pltpu.make_async_copy(ref, ref, sem).wait()
    feat_copy.wait()
    red_copy.wait()


def local(latent, conv_weights, conv_bias, norm_gain, norm_shift, time_shift):
    vmem, anywhere = pl.BlockSpec(memory_space=pltpu.VMEM), pl.BlockSpec(memory_space=pl.ANY)
    return pl.pallas_call(
        kernel,
        out_shape=(
            jax.ShapeDtypeStruct((TH, TW, C), bf16),
            jax.ShapeDtypeStruct((TH // 2, TW // 2, C), bf16),
        ),
        in_specs=[anywhere, anywhere, vmem, vmem, vmem, vmem],
        out_specs=(anywhere, anywhere),
        scratch_shapes=[
            pltpu.VMEM((TH, TW, C), bf16),
            pltpu.VMEM((5, SHARD, C), bf16),
            pltpu.VMEM((TH + 2, TW, 384), bf16),
            pltpu.VMEM((TH + 2, TW, 384), bf16),
            pltpu.VMEM((TH + 2, TW, 384), bf16),
            pltpu.VMEM((TH + 2, TW, 128), bf16),
            pltpu.VMEM((2 * TH, 1024), bf16),
            pltpu.VMEM((8, RB, 80, 128), f32),
            pltpu.VMEM((8, RB, 80, 128), f32),
            pltpu.VMEM((5, 2, 3, 48, 128), f32),
            pltpu.VMEM((2, 3, 48, 128), f32),
            pltpu.VMEM((5, 2, 3, TH, 128), f32),
            pltpu.VMEM((5, 2, NR, 240, 128), bf16),
            pltpu.VMEM((2, 1024, 1024), bf16),
            pltpu.VMEM((384, 128), bf16),
            pltpu.VMEM((128, 384), bf16),
            pltpu.VMEM((6, 1, 128), f32),
            pltpu.VMEM((4, NR * NCOL - 1, 1, 128), f32),
            pltpu.VMEM((NR + NCOL - 2, 1, 128), f32),
            pltpu.VMEM((TH, TW, C), bf16),
            pltpu.VMEM((TH // 2, TW // 2, C), bf16),
            pltpu.SemaphoreType.DMA((5,)),
            pltpu.SemaphoreType.DMA((2,)),
            pltpu.SemaphoreType.DMA((5, 3)),
            pltpu.SemaphoreType.DMA((5, 3)),
            pltpu.SemaphoreType.DMA((5, 8)),
            pltpu.SemaphoreType.DMA((5, 8)),
            pltpu.SemaphoreType.DMA((6,)),
            pltpu.SemaphoreType.DMA((6,)),
        ],
        compiler_params=pltpu.CompilerParams(
            collective_id=0, has_side_effects=True, vmem_limit_bytes=60 * 1024 * 1024
        ),
        name="down_block",
    )(latent, conv_weights, conv_bias, norm_gain, norm_shift, time_shift)


def solution(mesh):
    split = Mesh(mesh.devices.reshape(NY, NX, NZ, NC), ("rows_0", "rows_1", "cols_0", "cols_1"))
    placed = (P(ROWS, COLS, None), P(None, ROWS, None), P(), P(), P(), P())
    return jax.shard_map(
        local,
        mesh=split,
        in_specs=placed,
        out_specs=(P(ROWS, COLS, None), P(ROWS, COLS, None)),
        check_vma=False,
    )
```

```python
import functools
import itertools

import jax
import jax.numpy as jnp
from jax import lax
from jax.experimental import pallas as pl
from jax.experimental.pallas import tpu as pltpu
from jax.sharding import Mesh
from jax.sharding import PartitionSpec as P

f32, bf16 = jnp.float32, jnp.bfloat16
MESH = pl.DeviceIdType.MESH
ROWS = ("rows_0", "rows_1")
COLS = ("cols_0", "cols_1")
NY, NX, NZ, NC = 4, 4, 4, 2
NR, NCOL = NY * NX, NZ * NC
C = 320
TH, TW = 32, 64
SHARD = 180
RB = 8
NB = TH // RB
EPS = 1e-05


def padded(row, width=384):
    return jnp.concatenate([row, jnp.zeros((row.shape[0], width - row.shape[1]), row.dtype)], axis=1)


def window_tiles():
    tiles = []
    for tile in range(9 * C // 16):
        holders = []
        for r in range(NR):
            first = SHARD * r // 16
            last = (SHARD * (r + 1) - 1) // 16
            if first <= tile <= last:
                holders.append((r, tile - first))
        tiles.append(holders)
    return tiles


WINDOWS = window_tiles()


def others():
    sizes = (NY, NX, NZ, NC)
    steps = [o for o in itertools.product(*[range(n) for n in sizes]) if any(o)]
    return sorted(steps, key=lambda o: -sum(2 * min(v, n - v) for v, n in zip(o[:3], sizes)) - o[3])


OTHERS = others()


def kernel(
    lat_hbm, w_hbm, bias_ref, gain_ref, shift_ref, time_ref,
    feat_hbm, red_hbm,
    lat, wl, act_a, act_b, xs, r0, edge_mat, zs_even, zs_odd, hc, es, cs, gath, wk, to_group, to_channel,
    ar_src, ar_got, ar_first, fbuf, rbuf,
    sem_in, sem_out, ws_send, ws_recv, halo_send, halo_recv, ar_send, ar_recv,
):
    y, x = lax.axis_index("rows_0"), lax.axis_index("rows_1")
    z, core = lax.axis_index("cols_0"), lax.axis_index("cols_1")
    r, c = y * NX + x, z * NC + core

    def dev(rr, cc):
        return (rr // NX, lax.rem(rr, NX), cc // NC, lax.rem(cc, NC))

    def row_peer(j):
        return dev(lax.rem(r + j, NR), c)

    def col_peer(j):
        return dev(r, lax.rem(c + j, NCOL))

    up, down = lax.rem(r + NR - 1, NR), lax.rem(r + 1, NR)
    left, right = lax.rem(c + NCOL - 1, NCOL), lax.rem(c + 1, NCOL)

    lat_copies = []
    for i in range(4):
        cp = pltpu.make_async_copy(lat_hbm.at[pl.ds(8 * i, 8)], lat.at[pl.ds(8 * i, 8)], sem_in.at[i])
        cp.start()
        lat_copies.append(cp)
    w_copy = pltpu.make_async_copy(w_hbm, wl, sem_in.at[4])
    w_copy.start()

    barrier = pltpu.get_barrier_semaphore()
    peers = [row_peer(j) for j in range(1, NR)] + [col_peer(j) for j in range(1, NCOL)]
    for peer in peers:
        pl.semaphore_signal(barrier, inc=1, device_id=peer, device_id_type=MESH)

    major = jnp.where(core == 0, y, x)
    minor = jnp.where(core == 0, x, y)
    slot = 4 * major + minor
    w_copy.wait()
    off = lax.rem(4 * r, 16)
    row_id = lax.broadcasted_iota(jnp.int32, (96, SHARD), 0) + 96 * core
    col_id = lax.broadcasted_iota(jnp.int32, (96, SHARD), 1) + off
    place = jnp.where(row_id == col_id, 1.0, 0.0).astype(bf16)

    def prepare(k):
        half = jnp.dot(place, wl[k], preferred_element_type=f32)
        gath[k, core, slot, 0:96] = half[:, 0:128].astype(bf16)
        gath[k, core, slot, 96:192] = half[:, 128:256].astype(bf16)
        tail = jnp.concatenate([half[0:48, 256:320], half[48:96, 256:320]], axis=1)
        gath[k, core, slot, 192:240] = tail.astype(bf16)

    prepare(0)
    ci = lax.broadcasted_iota(jnp.int32, (384, 128), 0)
    gi = lax.broadcasted_iota(jnp.int32, (384, 128), 1)
    to_group[...] = jnp.where(((ci * 6554) >> 16) == gi, 1.0, 0.0).astype(bf16)
    ci = lax.broadcasted_iota(jnp.int32, (128, 384), 1)
    gi = lax.broadcasted_iota(jnp.int32, (128, 384), 0)
    to_channel[...] = jnp.where(((ci * 6554) >> 16) == gi, 1.0, 0.0).astype(bf16)


    def along(step_minor, step_major):
        mi = lax.rem(minor + step_minor, 4)
        ma = lax.rem(major + step_major, 4)
        return (jnp.where(core == 0, ma, mi), jnp.where(core == 0, mi, ma), z, core)

    pending_sends = []

    def w_stage1(k):
        mine = gath.at[k, core, slot]
        for j in range(1, 4):
            pltpu.make_async_remote_copy(mine, mine, ws_send.at[k, 0], ws_recv.at[k, 0], along(j, 0), MESH).start()
        pending_sends.append((gath.at[k, 0, 0:3], ws_send.at[k, 0]))

    def w_stage2(k):
        three = gath.at[k, 0, 0:3]
        pltpu.make_async_copy(three, three, ws_recv.at[k, 0]).wait()
        mine = gath.at[k, core, pl.ds(4 * major, 4)]
        for j in range(1, 4):
            pltpu.make_async_remote_copy(mine, mine, ws_send.at[k, 1], ws_recv.at[k, 1], along(0, j), MESH).start()
        pending_sends.append((gath.at[k, 0, 0:12], ws_send.at[k, 1]))

    def w_swap(k):
        twelve = gath.at[k, 0, 0:12]
        pltpu.make_async_copy(twelve, twelve, ws_recv.at[k, 1]).wait()
        mine = gath.at[k, core]
        pltpu.make_async_remote_copy(
            mine, mine, ws_send.at[k, 2], ws_recv.at[k, 2], (y, x, z, 1 - core), MESH
        ).start()
        pending_sends.append((gath.at[k, 0], ws_send.at[k, 2]))

    def w_arrived(k):
        every = gath.at[k, 0]
        pltpu.make_async_copy(every, every, ws_recv.at[k, 2]).wait()


    lane = lax.broadcasted_iota(jnp.int32, (1, 128), 1)
    low = lane < 64

    def relayout(k):
        wbuf = wk.at[k % 2]

        def piece(holder, part):
            rr, l = holder
            h, l6 = l // 6, l % 6
            s = rr if h == 0 else (rr % NX) * NY + rr // NX
            if part < 2:
                return gath[k, h, s, 96 * part + 16 * l6 : 96 * part + 16 * l6 + 16]
            t = gath[k, h, s, 192 + 16 * (l6 % 3) : 208 + 16 * (l6 % 3)].astype(f32)
            return t if l6 < 3 else pltpu.roll(t, 64, 1)

        def tile(t, part):
            return functools.reduce(lambda p, q: p + q, [piece(h, part) for h in WINDOWS[t]])

        for a in range(3):
            for u in range(20):
                row = 256 * a + 16 * u if u < 16 else 768 + 64 * a + 16 * (u - 16)
                tails = []
                for b in range(3):
                    t = 20 * (3 * a + b) + u
                    for part in range(2):
                        wbuf[row : row + 16, 256 * b + 128 * part : 256 * b + 128 * part + 128] = tile(t, part)
                    tails.append(jnp.where(low, tile(t, 2), 0.0))
                wbuf[row : row + 16, 768:896] = (tails[0] + pltpu.roll(tails[1], 64, 1)).astype(bf16)
                wbuf[row : row + 16, 896:1024] = tails[2].astype(bf16)

    zero_acc = tuple(jnp.zeros((8, 128), f32) for _ in range(6))

    def fold(v):
        return jnp.sum(v.reshape(v.shape[0] // 8, 8, 128), axis=0)

    def add_stats(acc, tiles):
        sums = [acc[t] + fold(tiles[t]) for t in range(3)]
        squares = [acc[3 + t] + fold(tiles[t] * tiles[t]) for t in range(3)]
        return tuple(sums + squares)

    def stage_cols(phase, row, tiles):
        for t in range(3):
            cs[phase, 0, t, pl.ds(row, 1), :] = tiles[t][0:1]
            cs[phase, 1, t, pl.ds(row, 1), :] = tiles[t][63:64]

    def halo_messages(phase, act):
        msgs = [
            (act.at[TH], act.at[0], dev(down, c)),
            (cs.at[phase, 1], hc.at[phase, 0, :, 8:40, :], dev(r, right)),
            (cs.at[phase, 1, :, 24:32, :], hc.at[phase, 0, :, 0:8, :], dev(down, right)),
        ]
        if phase < 4:
            msgs += [
                (act.at[1], act.at[TH + 1], dev(up, c)),
                (cs.at[phase, 0], hc.at[phase, 1, :, 8:40, :], dev(r, left)),
                (cs.at[phase, 0, :, 24:32, :], hc.at[phase, 1, :, 0:8, :], dev(down, left)),
                (cs.at[phase, 1, :, 0:8, :], hc.at[phase, 0, :, 40:48, :], dev(up, right)),
                (cs.at[phase, 0, :, 0:8, :], hc.at[phase, 1, :, 40:48, :], dev(up, left)),
            ]
        return [
            pltpu.make_async_remote_copy(s, d, halo_send.at[phase, i], halo_recv.at[phase, i], to, MESH)
            for i, (s, d, to) in enumerate(msgs)
        ]

    def thirds(v):
        hi = v.astype(bf16).astype(f32)
        mid = (v - hi).astype(bf16).astype(f32)
        return jnp.concatenate([hi, mid, v - hi - mid], axis=0).astype(bf16)

    def own_sums(acc):
        sums = jnp.concatenate(
            [jnp.concatenate(acc[0:3], axis=1), jnp.concatenate(acc[3:6], axis=1)], axis=0
        )
        got = jnp.dot(thirds(sums), to_group[...], preferred_element_type=f32)
        got = got[0:16] + got[16:32] + got[32:48]
        return jnp.sum(got[0:8], axis=0, keepdims=True) + pltpu.roll(jnp.sum(got[8:16], axis=0, keepdims=True), 32, 1)

    def send_sums(phase, own):
        ar_src[phase] = own
        me = (y, x, z, core)
        for j, offset in enumerate(OTHERS):
            to = tuple(lax.rem(m + o, n) if o else m for m, o, n in zip(me, offset, (NY, NX, NZ, NC)))
            pltpu.make_async_remote_copy(
                ar_src.at[phase], ar_got.at[phase, j], ar_send.at[phase], ar_recv.at[phase], to, MESH
            ).start()
        pending_sends.append((ar_got.at[phase], ar_send.at[phase]))

    def first_sums(own, between):
        at = 0
        for stage, (peer, n) in enumerate(((col_peer, NCOL), (row_peer, NR))):
            ar_src[4 + stage] = own
            got = ar_first.at[pl.ds(at, n - 1)]
            for j in range(1, n):
                pltpu.make_async_remote_copy(
                    ar_src.at[4 + stage], ar_first.at[at + j - 1], ar_send.at[4 + stage], ar_recv.at[4 + stage], peer(j), MESH
                ).start()
            pending_sends.append((got, ar_send.at[4 + stage]))
            between[stage]()
            pltpu.make_async_copy(got, got, ar_recv.at[4 + stage]).wait()
            own = own + jnp.sum(ar_first[at : at + n - 1], axis=0)
            at += n - 1
        return own

    def all_sums(phase, own):
        every = ar_got.at[phase]
        pltpu.make_async_copy(every, every, ar_recv.at[phase]).wait()
        return own + jnp.sum(ar_got[phase], axis=0)

    def scales(phase, vec):
        count = float(TH * NR * TW * NCOL * (C // 32))
        mean = vec / count
        spread = jnp.maximum(pltpu.roll(mean, 96, 1) - mean * mean, 0.0)
        scale = lax.rsqrt(spread + EPS)
        pair = jnp.concatenate([scale, mean * scale], axis=0)
        pair = jnp.where(lane < 32, pair, 0.0)
        tot = jnp.dot(thirds(jnp.concatenate([pair, jnp.zeros((6, 128), f32)], axis=0)), to_channel[...], preferred_element_type=f32)
        tot = tot[0:8] + tot[8:16] + tot[16:24]
        gain = padded(0.5 * gain_ref[phase : phase + 1, :])
        scale = tot[0:1] * gain
        move = padded(0.5 * shift_ref[phase : phase + 1, :]) - tot[1:2] * gain
        return [scale[:, 128 * t : 128 * t + 128] for t in range(3)], [move[:, 128 * t : 128 * t + 128] for t in range(3)]

    def silu_of(v, scale, move):
        half = v * scale + move
        return half + half * jnp.tanh(half)

    def on(cond):
        return jnp.where(cond, 1.0, 0.0).astype(f32)

    top, bottom = on(r > 0), on(r < NR - 1)
    west, east = on(c > 0), on(c < NCOL - 1)

    def edge_taps(side, rows, stride):
        def tap(t, a):
            if stride > 1:
                return es[side, t, pl.ds(7 + a, rows, stride=stride), :]
            return es[side, t, 7 + a : 7 + a + rows, :]

        cols = [tap(t, a) for a in range(3) for t in range(2)]
        return cols + [tap(2, 0) + pltpu.roll(tap(2, 1), 64, 1), tap(2, 2)]

    def edges_to_matrix():
        both = [edge_taps(side, TH, 1) for side in range(2)]
        for b in range(NB):
            for i in range(8):
                pair = [both[side][i][RB * b : RB * b + RB] for side in range(2)]
                edge_mat[2 * RB * b : 2 * RB * (b + 1), 128 * i : 128 * i + 128] = jnp.concatenate(pair, axis=0).astype(bf16)

    er = lax.broadcasted_iota(jnp.int32, (48, 1), 0)
    edge_rows = jnp.where(er < 8, top, jnp.where(er < 40, 1.0, bottom))

    def norm_rows(act, sc, mv, carry, rows):
        for i in reversed(rows):
            tiles = []
            for t in range(3):
                scale, move = sc[t], mv[t]
                if i in (0, TH + 1):
                    mask = top if i == 0 else bottom
                    scale, move = scale * mask, move * mask
                v = act[i, :, 128 * t : 128 * t + 128].astype(f32)
                tiles.append(silu_of(v, scale, move))
                xs[i, :, 128 * t : 128 * t + 128] = tiles[t].astype(bf16)
            if carry[0] is not None:
                r0[i + 1] = (tiles[2] + carry[0]).astype(bf16)
            carry[0] = pltpu.roll(tiles[2], 64, 1)

    def norm_edges(phase, sc, mv):
        for side, mask in ((0, west), (1, east)):
            for t in range(3):
                es[side, t] = silu_of(hc[phase, side, t], sc[t], mv[t]) * (edge_rows * mask)
        edges_to_matrix()

    def block_dot(k, zs, parts, edges, work):
        lhs = jnp.concatenate([jnp.concatenate(parts, axis=1), edges], axis=0)
        rows = RB * TW
        for n in range(4):
            o = jnp.dot(lhs, wk[k % 2, :, 256 * n : 256 * n + 256], preferred_element_type=f32)
            for t in range(2):
                p = o[:, 128 * t : 128 * t + 128]
                tile = 2 * n + t
                zs[tile, :, 8 : 8 + TW, :] = p[0:rows].reshape(RB, TW, 128)
                if tile in (0, 1, 6):
                    for rr in range(RB):
                        zs[tile, rr, 7:8, :] = p[rows + rr : rows + rr + 1]
                if tile in (4, 5, 7):
                    for rr in range(RB):
                        zs[tile, rr, 8 + TW : 9 + TW, :] = p[rows + RB + rr : rows + RB + rr + 1]
            for item in work[len(work) * n // 4 : len(work) * (n + 1) // 4]:
                item()

    def taps_sum(zs, rr, width, stride):
        def at(t, first):
            if stride > 1:
                return zs[t, rr, pl.ds(first, width, stride=stride), :]
            return zs[t, rr, first : first + width, :]

        outs = [at(t, 7) + at(2 + t, 8) + at(4 + t, 9) for t in range(2)]
        tail = at(6, 7) + pltpu.roll(at(6, 8), 64, 1) + at(7, 9)
        return outs + [jnp.where(low, tail, 0.0)]

    def split(row):
        row = padded(row)
        return [row[:, 128 * t : 128 * t + 128] for t in range(3)]

    def convolve(k, act, sc, mv, res, out, ahead, hooks):
        extra = split(bias_ref[k : k + 1, :] + (time_ref[k // 2 : k // 2 + 1, :] if k % 2 == 0 else 0.0))
        stats = [zero_acc]
        carry = [None]

        def norm_item(rows):
            return lambda: norm_rows(act, sc, mv, carry, rows)

        def needed(b):
            return range(RB * b, RB * b + RB if b < NB - 1 else TH + 2)

        def finish_row(zs, b, rr):
            row = RB * b + rr
            tiles = []
            for t, o in enumerate(taps_sum(zs, rr, TW, 1)):
                o = o + extra[t]
                if res is not None:
                    o = o + res[row + 1, :, 128 * t : 128 * t + 128].astype(f32)
                o = o.astype(bf16)
                out[row + 1, :, 128 * t : 128 * t + 128] = o
                tiles.append(o.astype(f32))
            for t in range(3):
                cs[k + 1, 0, t, row : row + 1, :] = tiles[t][0:1]
                cs[k + 1, 1, t, row : row + 1, :] = tiles[t][TW - 1 : TW]
            if k == 3:
                fbuf[row] = jnp.concatenate([tiles[0], tiles[1], tiles[2][:, 0:64]], axis=1).astype(bf16)
            else:
                stats[0] = add_stats(stats[0], tiles)

        def finish_item(zs, b, rr):
            return lambda: finish_row(zs, b, rr)

        norm_rows(act, sc, mv, carry, needed(NB - 1))
        if ahead is not None:
            ahead[0]()
            norm_rows(act, sc, mv, carry, range(0, RB * (NB - 1)))
            ahead[1]()
        before = []
        for step, b in enumerate(reversed(range(NB))):
            zs = zs_even if step % 2 == 0 else zs_odd
            if step in hooks:
                hooks[step]()
            parts = [xs[RB * b + a : RB * b + a + RB, :, 0:256].reshape(RB * TW, 256) for a in range(3)]
            parts.append(r0[RB * b + 1 : RB * b + 1 + RB].reshape(RB * TW, 128))
            parts.append(xs[RB * b + 2 : RB * b + 2 + RB, :, 256:384].reshape(RB * TW, 128))
            work = list(before)
            if b > 0 and ahead is None:
                norms = [norm_item(range(i, i + 1)) for i in reversed(needed(b - 1))]
                work = [w for pair in itertools.zip_longest(norms, work) for w in pair if w is not None]
            block_dot(k, zs, parts, edge_mat[2 * RB * b : 2 * RB * (b + 1)], work)
            before = [finish_item(zs, b, rr) for rr in reversed(range(RB))]
        for item in before:
            item()
        return stats[0]

    def read_latent(i, acc):
        v = lat[i].astype(f32)
        tiles = [v[:, 0:128], v[:, 128:256], padded(v[:, 256:320], 128)]
        for t in range(3):
            act_a[i + 1, :, 128 * t : 128 * t + 128] = tiles[t].astype(bf16)
        stage_cols(0, i, tiles)
        return add_stats(acc, tiles)

    acc = zero_acc
    for i in range(4):
        lat_copies[i].wait()
        acc = lax.fori_loop(8 * i, 8 * i + 8, read_latent, acc)


    pl.semaphore_wait(barrier, len(peers))
    w_stage1(0)

    for k in range(4):
        act, res, out = (act_a, None, act_b) if k % 2 == 0 else (act_b, act_a, act_a)
        own = own_sums(acc)
        halos = halo_messages(k, act)
        straight = [h for i, h in enumerate(halos) if i in (0, 1, 3, 4)]
        corners = [h for i, h in enumerate(halos) if i in (2, 5, 6, 7)]
        ahead = None
        if k == 0:
            def beside_first():
                for h in straight:
                    h.start()
                for later in range(1, 5):
                    prepare(later)
                for i in range(2):
                    wk[i, 960:1024, :] = jnp.zeros((64, 1024), bf16)

            def beside_second():
                for h in corners:
                    h.start()
                w_stage2(0)
                w_stage1(1)

            def got_first():
                w_arrived(0)
                w_stage2(1)
                relayout(0)

            ahead = (functools.partial(w_swap, 0), got_first)
            total = first_sums(own, (beside_first, beside_second))
        else:
            send_sums(k, own)
            for h in straight + corners:
                h.start()
            w_swap(k)
            if k == 3:
                w_stage2(4)
            else:
                w_stage1(k + 1)
                if k == 2:
                    w_stage1(4)
            w_arrived(k)
            relayout(k)
            total = all_sums(k, own)
        sc, mv = scales(k, total)
        for h in halos:
            h.wait()
        norm_edges(k, sc, mv)
        hooks = {}
        if k in (1, 2):
            w_stage2(k + 1)
        if k == 3:
            last_halos = halo_messages(4, act_a)

            def lowest_row_done():
                last_halos[0].start()
                last_halos[2].start()

            def last_weights():
                w_arrived(4)
                relayout(4)

            hooks = {1: functools.partial(w_swap, 4), 2: lowest_row_done, 3: last_weights}
        acc = convolve(k, act, sc, mv, res, out, ahead, hooks)

    last_halos[1].start()
    feat_copy = pltpu.make_async_copy(fbuf, feat_hbm, sem_out.at[0])
    feat_copy.start()
    half = TH // 2
    extra4 = split(bias_ref[4:5, :])

    def reduced_parts(b):
        def every_other(first, lanes):
            return jnp.concatenate([act_a[2 * p + first, :, lanes] for p in range(RB * b, RB * b + RB)], axis=0)

        heads = [every_other(a, slice(0, 256)) for a in range(3)]
        pair = every_other(0, slice(256, 384)).astype(f32) + pltpu.roll(every_other(1, slice(256, 384)).astype(f32), 64, 1)
        return heads + [pair.astype(bf16), every_other(2, slice(256, 384))]

    def dot4(zs, parts, edges):
        lhs = jnp.concatenate(parts, axis=1)
        rows = RB * TW
        if edges is not None:
            lhs = jnp.concatenate([lhs, edges], axis=0)
        for n in range(4):
            o = jnp.dot(lhs, wk[0, :, 256 * n : 256 * n + 256], preferred_element_type=f32)
            for t in range(2):
                tile = 2 * n + t
                p = o[:, 128 * t : 128 * t + 128]
                zs[tile, :, 8 : 8 + TW, :] = p[0:rows].reshape(RB, TW, 128)
                if edges is not None and tile in (0, 1, 6):
                    for rr in range(half):
                        (zs_odd if rr < RB else zs_even)[tile, rr % RB, 7:8, :] = p[rows + rr : rows + rr + 1]

    dot4(zs_even, reduced_parts(1), None)
    for h in last_halos:
        h.wait()
    for t in range(3):
        act_a[0, :, 128 * t : 128 * t + 128] = (act_a[0, :, 128 * t : 128 * t + 128].astype(f32) * top).astype(bf16)
        es[0, t] = hc[4, 0, t] * (edge_rows * west)
    left_taps = jnp.concatenate(edge_taps(0, half, 2), axis=1).astype(bf16)
    dot4(zs_odd, reduced_parts(0), left_taps)

    def last(zs, first):
        def one(p, carry):
            tiles = [o + extra4[t] for t, o in enumerate(taps_sum(zs, p, TW // 2, 2))]
            rbuf[first + p] = jnp.concatenate([tiles[0], tiles[1], tiles[2][:, 0:64]], axis=1).astype(bf16)
            return carry

        lax.fori_loop(0, RB, one, 0)

    last(zs_even, RB)
    last(zs_odd, 0)
    red_copy = pltpu.make_async_copy(rbuf, red_hbm, sem_out.at[1])
    red_copy.start()
    for ref, sem in pending_sends:
        pltpu.make_async_copy(ref, ref, sem).wait()
    feat_copy.wait()
    red_copy.wait()


def local(latent, conv_weights, conv_bias, norm_gain, norm_shift, time_shift):
    vmem, anywhere = pl.BlockSpec(memory_space=pltpu.VMEM), pl.BlockSpec(memory_space=pl.ANY)
    return pl.pallas_call(
        kernel,
        out_shape=(
            jax.ShapeDtypeStruct((TH, TW, C), bf16),
            jax.ShapeDtypeStruct((TH // 2, TW // 2, C), bf16),
        ),
        in_specs=[anywhere, anywhere, vmem, vmem, vmem, vmem],
        out_specs=(anywhere, anywhere),
        scratch_shapes=[
            pltpu.VMEM((TH, TW, C), bf16),
            pltpu.VMEM((5, SHARD, C), bf16),
            pltpu.VMEM((TH + 2, TW, 384), bf16),
            pltpu.VMEM((TH + 2, TW, 384), bf16),
            pltpu.VMEM((TH + 2, TW, 384), bf16),
            pltpu.VMEM((TH + 2, TW, 128), bf16),
            pltpu.VMEM((2 * TH, 1024), bf16),
            pltpu.VMEM((8, RB, 80, 128), f32),
            pltpu.VMEM((8, RB, 80, 128), f32),
            pltpu.VMEM((5, 2, 3, 48, 128), f32),
            pltpu.VMEM((2, 3, 48, 128), f32),
            pltpu.VMEM((5, 2, 3, TH, 128), f32),
            pltpu.VMEM((5, 2, NR, 240, 128), bf16),
            pltpu.VMEM((2, 1024, 1024), bf16),
            pltpu.VMEM((384, 128), bf16),
            pltpu.VMEM((128, 384), bf16),
            pltpu.VMEM((6, 1, 128), f32),
            pltpu.VMEM((4, NR * NCOL - 1, 1, 128), f32),
            pltpu.VMEM((NR + NCOL - 2, 1, 128), f32),
            pltpu.VMEM((TH, TW, C), bf16),
            pltpu.VMEM((TH // 2, TW // 2, C), bf16),
            pltpu.SemaphoreType.DMA((5,)),
            pltpu.SemaphoreType.DMA((2,)),
            pltpu.SemaphoreType.DMA((5, 3)),
            pltpu.SemaphoreType.DMA((5, 3)),
            pltpu.SemaphoreType.DMA((5, 8)),
            pltpu.SemaphoreType.DMA((5, 8)),
            pltpu.SemaphoreType.DMA((6,)),
            pltpu.SemaphoreType.DMA((6,)),
        ],
        compiler_params=pltpu.CompilerParams(
            collective_id=0, has_side_effects=True, vmem_limit_bytes=60 * 1024 * 1024
        ),
        name="down_block",
    )(latent, conv_weights, conv_bias, norm_gain, norm_shift, time_shift)


def solution(mesh):
    split = Mesh(mesh.devices.reshape(NY, NX, NZ, NC), ("rows_0", "rows_1", "cols_0", "cols_1"))
    placed = (P(ROWS, COLS, None), P(None, ROWS, None), P(), P(), P(), P())
    return jax.shard_map(
        local,
        mesh=split,
        in_specs=placed,
        out_specs=(P(ROWS, COLS, None), P(ROWS, COLS, None)),
        check_vma=False,
    )
```

```python
import functools
import itertools

import jax
import jax.numpy as jnp
from jax import lax
from jax.experimental import pallas as pl
from jax.experimental.pallas import tpu as pltpu
from jax.sharding import Mesh
from jax.sharding import PartitionSpec as P

f32, bf16 = jnp.float32, jnp.bfloat16
MESH = pl.DeviceIdType.MESH
ROWS = ("rows_0", "rows_1")
COLS = ("cols_0", "cols_1")
NY, NX, NZ, NC = 4, 4, 4, 2
NR, NCOL = NY * NX, NZ * NC
C = 320
TH, TW = 32, 64
SHARD = 180
RB = 8
NB = TH // RB
EPS = 1e-05


def padded(row, width=384):
    return jnp.concatenate([row, jnp.zeros((row.shape[0], width - row.shape[1]), row.dtype)], axis=1)


def window_tiles():
    tiles = []
    for tile in range(9 * C // 16):
        holders = []
        for r in range(NR):
            first = SHARD * r // 16
            last = (SHARD * (r + 1) - 1) // 16
            if first <= tile <= last:
                holders.append((r, tile - first))
        tiles.append(holders)
    return tiles


WINDOWS = window_tiles()


def others():
    sizes = (NY, NX, NZ, NC)
    steps = [o for o in itertools.product(*[range(n) for n in sizes]) if any(o)]
    return sorted(steps, key=lambda o: -sum(2 * min(v, n - v) for v, n in zip(o[:3], sizes)) - o[3])


OTHERS = others()


def kernel(
    lat_hbm, w_hbm, bias_ref, gain_ref, shift_ref, time_ref,
    feat_hbm, red_hbm,
    lat, wl, act_a, act_b, xs, r0, edge_mat, zs_even, zs_odd, hc, es, cs, gath, wk, to_group, to_channel,
    ar_src, ar_got, ar_first, fbuf, rbuf,
    sem_in, sem_out, ws_send, ws_recv, halo_send, halo_recv, ar_send, ar_recv,
):
    y, x = lax.axis_index("rows_0"), lax.axis_index("rows_1")
    z, core = lax.axis_index("cols_0"), lax.axis_index("cols_1")
    r, c = y * NX + x, z * NC + core

    def dev(rr, cc):
        return (rr // NX, lax.rem(rr, NX), cc // NC, lax.rem(cc, NC))

    def row_peer(j):
        return dev(lax.rem(r + j, NR), c)

    def col_peer(j):
        return dev(r, lax.rem(c + j, NCOL))

    up, down = lax.rem(r + NR - 1, NR), lax.rem(r + 1, NR)
    left, right = lax.rem(c + NCOL - 1, NCOL), lax.rem(c + 1, NCOL)

    lat_copies = []
    for i in range(4):
        cp = pltpu.make_async_copy(lat_hbm.at[pl.ds(8 * i, 8)], lat.at[pl.ds(8 * i, 8)], sem_in.at[i])
        cp.start()
        lat_copies.append(cp)
    w_copy = pltpu.make_async_copy(w_hbm, wl, sem_in.at[4])
    w_copy.start()

    barrier = pltpu.get_barrier_semaphore()
    peers = [row_peer(j) for j in range(1, NR)] + [col_peer(j) for j in range(1, NCOL)]
    for peer in peers:
        pl.semaphore_signal(barrier, inc=1, device_id=peer, device_id_type=MESH)

    major = jnp.where(core == 0, y, x)
    minor = jnp.where(core == 0, x, y)
    slot = 4 * major + minor
    w_copy.wait()
    off = lax.rem(4 * r, 16)
    row_id = lax.broadcasted_iota(jnp.int32, (96, SHARD), 0) + 96 * core
    col_id = lax.broadcasted_iota(jnp.int32, (96, SHARD), 1) + off
    place = jnp.where(row_id == col_id, 1.0, 0.0).astype(bf16)

    def prepare(k):
        half = jnp.dot(place, wl[k], preferred_element_type=f32)
        gath[k, core, slot, 0:96] = half[:, 0:128].astype(bf16)
        gath[k, core, slot, 96:192] = half[:, 128:256].astype(bf16)
        tail = jnp.concatenate([half[0:48, 256:320], half[48:96, 256:320]], axis=1)
        gath[k, core, slot, 192:240] = tail.astype(bf16)

    prepare(0)
    ci = lax.broadcasted_iota(jnp.int32, (384, 128), 0)
    gi = lax.broadcasted_iota(jnp.int32, (384, 128), 1)
    to_group[...] = jnp.where(((ci * 6554) >> 16) == gi, 1.0, 0.0).astype(bf16)
    ci = lax.broadcasted_iota(jnp.int32, (128, 384), 1)
    gi = lax.broadcasted_iota(jnp.int32, (128, 384), 0)
    to_channel[...] = jnp.where(((ci * 6554) >> 16) == gi, 1.0, 0.0).astype(bf16)


    def along(step_minor, step_major):
        mi = lax.rem(minor + step_minor, 4)
        ma = lax.rem(major + step_major, 4)
        return (jnp.where(core == 0, ma, mi), jnp.where(core == 0, mi, ma), z, core)

    pending_sends = []

    def w_stage1(k):
        mine = gath.at[k, core, slot]
        for j in range(1, 4):
            pltpu.make_async_remote_copy(mine, mine, ws_send.at[k, 0], ws_recv.at[k, 0], along(j, 0), MESH).start()
        pending_sends.append((gath.at[k, 0, 0:3], ws_send.at[k, 0]))

    def w_stage2(k):
        three = gath.at[k, 0, 0:3]
        pltpu.make_async_copy(three, three, ws_recv.at[k, 0]).wait()
        mine = gath.at[k, core, pl.ds(4 * major, 4)]
        for j in range(1, 4):
            pltpu.make_async_remote_copy(mine, mine, ws_send.at[k, 1], ws_recv.at[k, 1], along(0, j), MESH).start()
        pending_sends.append((gath.at[k, 0, 0:12], ws_send.at[k, 1]))

    def w_swap(k):
        twelve = gath.at[k, 0, 0:12]
        pltpu.make_async_copy(twelve, twelve, ws_recv.at[k, 1]).wait()
        mine = gath.at[k, core]
        pltpu.make_async_remote_copy(
            mine, mine, ws_send.at[k, 2], ws_recv.at[k, 2], (y, x, z, 1 - core), MESH
        ).start()
        pending_sends.append((gath.at[k, 0], ws_send.at[k, 2]))

    def w_arrived(k):
        every = gath.at[k, 0]
        pltpu.make_async_copy(every, every, ws_recv.at[k, 2]).wait()


    lane = lax.broadcasted_iota(jnp.int32, (1, 128), 1)
    low = lane < 64

    def relayout(k):
        wbuf = wk.at[k % 2]

        def piece(holder, part):
            rr, l = holder
            h, l6 = l // 6, l % 6
            s = rr if h == 0 else (rr % NX) * NY + rr // NX
            if part < 2:
                return gath[k, h, s, 96 * part + 16 * l6 : 96 * part + 16 * l6 + 16]
            t = gath[k, h, s, 192 + 16 * (l6 % 3) : 208 + 16 * (l6 % 3)].astype(f32)
            return t if l6 < 3 else pltpu.roll(t, 64, 1)

        def tile(t, part):
            return functools.reduce(lambda p, q: p + q, [piece(h, part) for h in WINDOWS[t]])

        for a in range(3):
            for u in range(20):
                row = 256 * a + 16 * u if u < 16 else 768 + 64 * a + 16 * (u - 16)
                tails = []
                for b in range(3):
                    t = 20 * (3 * a + b) + u
                    for part in range(2):
                        wbuf[row : row + 16, 256 * b + 128 * part : 256 * b + 128 * part + 128] = tile(t, part)
                    tails.append(jnp.where(low, tile(t, 2), 0.0))
                wbuf[row : row + 16, 768:896] = (tails[0] + pltpu.roll(tails[1], 64, 1)).astype(bf16)
                wbuf[row : row + 16, 896:1024] = tails[2].astype(bf16)

    zero_acc = tuple(jnp.zeros((8, 128), f32) for _ in range(6))

    def fold(v):
        return jnp.sum(v.reshape(v.shape[0] // 8, 8, 128), axis=0)

    def add_stats(acc, tiles):
        sums = [acc[t] + fold(tiles[t]) for t in range(3)]
        squares = [acc[3 + t] + fold(tiles[t] * tiles[t]) for t in range(3)]
        return tuple(sums + squares)

    def stage_cols(phase, row, tiles):
        for t in range(3):
            cs[phase, 0, t, pl.ds(row, 1), :] = tiles[t][0:1]
            cs[phase, 1, t, pl.ds(row, 1), :] = tiles[t][63:64]

    def halo_messages(phase, act):
        msgs = [
            (act.at[TH], act.at[0], dev(down, c)),
            (cs.at[phase, 1], hc.at[phase, 0, :, 8:40, :], dev(r, right)),
            (cs.at[phase, 1, :, 24:32, :], hc.at[phase, 0, :, 0:8, :], dev(down, right)),
        ]
        if phase < 4:
            msgs += [
                (act.at[1], act.at[TH + 1], dev(up, c)),
                (cs.at[phase, 0], hc.at[phase, 1, :, 8:40, :], dev(r, left)),
                (cs.at[phase, 0, :, 24:32, :], hc.at[phase, 1, :, 0:8, :], dev(down, left)),
                (cs.at[phase, 1, :, 0:8, :], hc.at[phase, 0, :, 40:48, :], dev(up, right)),
                (cs.at[phase, 0, :, 0:8, :], hc.at[phase, 1, :, 40:48, :], dev(up, left)),
            ]
        return [
            pltpu.make_async_remote_copy(s, d, halo_send.at[phase, i], halo_recv.at[phase, i], to, MESH)
            for i, (s, d, to) in enumerate(msgs)
        ]

    def thirds(v):
        hi = v.astype(bf16).astype(f32)
        mid = (v - hi).astype(bf16).astype(f32)
        return jnp.concatenate([hi, mid, v - hi - mid], axis=0).astype(bf16)

    def own_sums(acc):
        sums = jnp.concatenate(
            [jnp.concatenate(acc[0:3], axis=1), jnp.concatenate(acc[3:6], axis=1)], axis=0
        )
        got = jnp.dot(thirds(sums), to_group[...], preferred_element_type=f32)
        got = got[0:16] + got[16:32] + got[32:48]
        return jnp.sum(got[0:8], axis=0, keepdims=True) + pltpu.roll(jnp.sum(got[8:16], axis=0, keepdims=True), 32, 1)

    def send_sums(phase, own):
        ar_src[phase] = own
        me = (y, x, z, core)
        for j, offset in enumerate(OTHERS):
            to = tuple(lax.rem(m + o, n) if o else m for m, o, n in zip(me, offset, (NY, NX, NZ, NC)))
            pltpu.make_async_remote_copy(
                ar_src.at[phase], ar_got.at[phase, j], ar_send.at[phase], ar_recv.at[phase], to, MESH
            ).start()
        pending_sends.append((ar_got.at[phase], ar_send.at[phase]))

    def first_sums(own, between):
        at = 0
        for stage, (peer, n) in enumerate(((col_peer, NCOL), (row_peer, NR))):
            ar_src[4 + stage] = own
            got = ar_first.at[pl.ds(at, n - 1)]
            for j in range(1, n):
                pltpu.make_async_remote_copy(
                    ar_src.at[4 + stage], ar_first.at[at + j - 1], ar_send.at[4 + stage], ar_recv.at[4 + stage], peer(j), MESH
                ).start()
            pending_sends.append((got, ar_send.at[4 + stage]))
            between[stage]()
            pltpu.make_async_copy(got, got, ar_recv.at[4 + stage]).wait()
            own = own + jnp.sum(ar_first[at : at + n - 1], axis=0)
            at += n - 1
        return own

    def all_sums(phase, own):
        every = ar_got.at[phase]
        pltpu.make_async_copy(every, every, ar_recv.at[phase]).wait()
        return own + jnp.sum(ar_got[phase], axis=0)

    def scales(phase, vec):
        count = float(TH * NR * TW * NCOL * (C // 32))
        mean = vec / count
        spread = jnp.maximum(pltpu.roll(mean, 96, 1) - mean * mean, 0.0)
        scale = lax.rsqrt(spread + EPS)
        pair = jnp.concatenate([scale, mean * scale], axis=0)
        pair = jnp.where(lane < 32, pair, 0.0)
        tot = jnp.dot(thirds(jnp.concatenate([pair, jnp.zeros((6, 128), f32)], axis=0)), to_channel[...], preferred_element_type=f32)
        tot = tot[0:8] + tot[8:16] + tot[16:24]
        gain = padded(0.5 * gain_ref[phase : phase + 1, :])
        scale = tot[0:1] * gain
        move = padded(0.5 * shift_ref[phase : phase + 1, :]) - tot[1:2] * gain
        return [scale[:, 128 * t : 128 * t + 128] for t in range(3)], [move[:, 128 * t : 128 * t + 128] for t in range(3)]

    def silu_of(v, scale, move):
        half = v * scale + move
        return half + half * jnp.tanh(half)

    def on(cond):
        return jnp.where(cond, 1.0, 0.0).astype(f32)

    top, bottom = on(r > 0), on(r < NR - 1)
    west, east = on(c > 0), on(c < NCOL - 1)

    def edge_taps(side, rows, stride):
        def tap(t, a):
            if stride > 1:
                return es[side, t, pl.ds(7 + a, rows, stride=stride), :]
            return es[side, t, 7 + a : 7 + a + rows, :]

        cols = [tap(t, a) for a in range(3) for t in range(2)]
        return cols + [tap(2, 0) + pltpu.roll(tap(2, 1), 64, 1), tap(2, 2)]

    def edges_to_matrix():
        both = [edge_taps(side, TH, 1) for side in range(2)]
        for b in range(NB):
            for i in range(8):
                pair = [both[side][i][RB * b : RB * b + RB] for side in range(2)]
                edge_mat[2 * RB * b : 2 * RB * (b + 1), 128 * i : 128 * i + 128] = jnp.concatenate(pair, axis=0).astype(bf16)

    er = lax.broadcasted_iota(jnp.int32, (48, 1), 0)
    edge_rows = jnp.where(er < 8, top, jnp.where(er < 40, 1.0, bottom))

    def norm_rows(act, sc, mv, carry, rows):
        for i in reversed(rows):
            tiles = []
            for t in range(3):
                scale, move = sc[t], mv[t]
                if i in (0, TH + 1):
                    mask = top if i == 0 else bottom
                    scale, move = scale * mask, move * mask
                v = act[i, :, 128 * t : 128 * t + 128].astype(f32)
                tiles.append(silu_of(v, scale, move))
                xs[i, :, 128 * t : 128 * t + 128] = tiles[t].astype(bf16)
            if carry[0] is not None:
                r0[i + 1] = (tiles[2] + carry[0]).astype(bf16)
            carry[0] = pltpu.roll(tiles[2], 64, 1)

    def norm_edges(phase, sc, mv):
        for side, mask in ((0, west), (1, east)):
            for t in range(3):
                es[side, t] = silu_of(hc[phase, side, t], sc[t], mv[t]) * (edge_rows * mask)
        edges_to_matrix()

    def block_dot(k, zs, parts, edges, work):
        lhs = jnp.concatenate([jnp.concatenate(parts, axis=1), edges], axis=0)
        rows = RB * TW
        for n in range(4):
            o = jnp.dot(lhs, wk[k % 2, :, 256 * n : 256 * n + 256], preferred_element_type=f32)
            for t in range(2):
                p = o[:, 128 * t : 128 * t + 128]
                tile = 2 * n + t
                zs[tile, :, 8 : 8 + TW, :] = p[0:rows].reshape(RB, TW, 128)
                if tile in (0, 1, 6):
                    for rr in range(RB):
                        zs[tile, rr, 7:8, :] = p[rows + rr : rows + rr + 1]
                if tile in (4, 5, 7):
                    for rr in range(RB):
                        zs[tile, rr, 8 + TW : 9 + TW, :] = p[rows + RB + rr : rows + RB + rr + 1]
            for item in work[len(work) * n // 4 : len(work) * (n + 1) // 4]:
                item()

    def taps_sum(zs, rr, width, stride):
        def at(t, first):
            if stride > 1:
                return zs[t, rr, pl.ds(first, width, stride=stride), :]
            return zs[t, rr, first : first + width, :]

        outs = [at(t, 7) + at(2 + t, 8) + at(4 + t, 9) for t in range(2)]
        tail = at(6, 7) + pltpu.roll(at(6, 8), 64, 1) + at(7, 9)
        return outs + [jnp.where(low, tail, 0.0)]

    def split(row):
        row = padded(row)
        return [row[:, 128 * t : 128 * t + 128] for t in range(3)]

    def convolve(k, act, sc, mv, res, out, ahead, hooks):
        extra = split(bias_ref[k : k + 1, :] + (time_ref[k // 2 : k // 2 + 1, :] if k % 2 == 0 else 0.0))
        stats = [zero_acc]
        carry = [None]

        def norm_item(rows):
            return lambda: norm_rows(act, sc, mv, carry, rows)

        def needed(b):
            return range(RB * b, RB * b + RB if b < NB - 1 else TH + 2)

        def finish_row(zs, b, rr):
            row = RB * b + rr
            tiles = []
            for t, o in enumerate(taps_sum(zs, rr, TW, 1)):
                o = o + extra[t]
                if res is not None:
                    o = o + res[row + 1, :, 128 * t : 128 * t + 128].astype(f32)
                o = o.astype(bf16)
                out[row + 1, :, 128 * t : 128 * t + 128] = o
                tiles.append(o.astype(f32))
            for t in range(3):
                cs[k + 1, 0, t, row : row + 1, :] = tiles[t][0:1]
                cs[k + 1, 1, t, row : row + 1, :] = tiles[t][TW - 1 : TW]
            if k == 3:
                fbuf[row] = jnp.concatenate([tiles[0], tiles[1], tiles[2][:, 0:64]], axis=1).astype(bf16)
            else:
                stats[0] = add_stats(stats[0], tiles)

        def finish_item(zs, b, rr):
            return lambda: finish_row(zs, b, rr)

        norm_rows(act, sc, mv, carry, needed(NB - 1))
        if ahead is not None:
            ahead[0]()
            norm_rows(act, sc, mv, carry, range(0, RB * (NB - 1)))
            ahead[1]()
        before = []
        for step, b in enumerate(reversed(range(NB))):
            zs = zs_even if step % 2 == 0 else zs_odd
            if step in hooks:
                hooks[step]()
            parts = [xs[RB * b + a : RB * b + a + RB, :, 0:256].reshape(RB * TW, 256) for a in range(3)]
            parts.append(r0[RB * b + 1 : RB * b + 1 + RB].reshape(RB * TW, 128))
            parts.append(xs[RB * b + 2 : RB * b + 2 + RB, :, 256:384].reshape(RB * TW, 128))
            work = list(before)
            if b > 0 and ahead is None:
                norms = [norm_item(range(i, i + 1)) for i in reversed(needed(b - 1))]
                work = [w for pair in itertools.zip_longest(norms, work) for w in pair if w is not None]
            block_dot(k, zs, parts, edge_mat[2 * RB * b : 2 * RB * (b + 1)], work)
            before = [finish_item(zs, b, rr) for rr in reversed(range(RB))]
        for item in before:
            item()
        return stats[0]

    def read_latent(i, acc):
        v = lat[i].astype(f32)
        tiles = [v[:, 0:128], v[:, 128:256], padded(v[:, 256:320], 128)]
        for t in range(3):
            act_a[i + 1, :, 128 * t : 128 * t + 128] = tiles[t].astype(bf16)
        stage_cols(0, i, tiles)
        return add_stats(acc, tiles)

    acc = zero_acc
    for i in range(4):
        lat_copies[i].wait()
        acc = lax.fori_loop(8 * i, 8 * i + 8, read_latent, acc)


    pl.semaphore_wait(barrier, len(peers))
    w_stage1(0)

    for k in range(4):
        act, res, out = (act_a, None, act_b) if k % 2 == 0 else (act_b, act_a, act_a)
        own = own_sums(acc)
        halos = halo_messages(k, act)
        straight = [h for i, h in enumerate(halos) if i in (0, 1, 3, 4)]
        corners = [h for i, h in enumerate(halos) if i in (2, 5, 6, 7)]
        ahead = None
        if k == 0:
            def beside_first():
                for h in straight:
                    h.start()
                for later in range(1, 5):
                    prepare(later)
                for i in range(2):
                    wk[i, 960:1024, :] = jnp.zeros((64, 1024), bf16)

            def beside_second():
                for h in corners:
                    h.start()
                w_stage2(0)
                w_stage1(1)

            def got_first():
                w_arrived(0)
                w_stage2(1)
                relayout(0)

            ahead = (functools.partial(w_swap, 0), got_first)
            total = first_sums(own, (beside_first, beside_second))
        else:
            send_sums(k, own)
            for h in straight + corners:
                h.start()
            w_swap(k)
            if k == 3:
                w_stage2(4)
            else:
                w_stage1(k + 1)
                if k == 2:
                    w_stage1(4)
            w_arrived(k)
            relayout(k)
            total = all_sums(k, own)
        sc, mv = scales(k, total)
        for h in halos:
            h.wait()
        norm_edges(k, sc, mv)
        hooks = {}
        if k in (1, 2):
            w_stage2(k + 1)
        if k == 3:
            last_halos = halo_messages(4, act_a)

            def lowest_row_done():
                last_halos[0].start()
                last_halos[2].start()

            def last_weights():
                w_arrived(4)
                relayout(4)

            hooks = {1: functools.partial(w_swap, 4), 2: lowest_row_done, 3: last_weights}
        acc = convolve(k, act, sc, mv, res, out, ahead, hooks)

    last_halos[1].start()
    feat_copy = pltpu.make_async_copy(fbuf, feat_hbm, sem_out.at[0])
    feat_copy.start()
    half = TH // 2
    extra4 = split(bias_ref[4:5, :])

    def reduced_parts(b):
        def every_other(first, lanes):
            return jnp.concatenate([act_a[2 * p + first, :, lanes] for p in range(RB * b, RB * b + RB)], axis=0)

        heads = [every_other(a, slice(0, 256)) for a in range(3)]
        pair = every_other(0, slice(256, 384)).astype(f32) + pltpu.roll(every_other(1, slice(256, 384)).astype(f32), 64, 1)
        return heads + [pair.astype(bf16), every_other(2, slice(256, 384))]

    def dot4(zs, parts, edges):
        lhs = jnp.concatenate(parts, axis=1)
        rows = RB * TW
        if edges is not None:
            lhs = jnp.concatenate([lhs, edges], axis=0)
        for n in range(4):
            o = jnp.dot(lhs, wk[0, :, 256 * n : 256 * n + 256], preferred_element_type=f32)
            for t in range(2):
                tile = 2 * n + t
                p = o[:, 128 * t : 128 * t + 128]
                zs[tile, :, 8 : 8 + TW, :] = p[0:rows].reshape(RB, TW, 128)
                if edges is not None and tile in (0, 1, 6):
                    for rr in range(half):
                        (zs_odd if rr < RB else zs_even)[tile, rr % RB, 7:8, :] = p[rows + rr : rows + rr + 1]

    dot4(zs_even, reduced_parts(1), None)
    for h in last_halos:
        h.wait()
    for t in range(3):
        act_a[0, :, 128 * t : 128 * t + 128] = (act_a[0, :, 128 * t : 128 * t + 128].astype(f32) * top).astype(bf16)
        es[0, t] = hc[4, 0, t] * (edge_rows * west)
    left_taps = jnp.concatenate(edge_taps(0, half, 2), axis=1).astype(bf16)
    dot4(zs_odd, reduced_parts(0), left_taps)

    def last(zs, first):
        def one(p, carry):
            tiles = [o + extra4[t] for t, o in enumerate(taps_sum(zs, p, TW // 2, 2))]
            rbuf[first + p] = jnp.concatenate([tiles[0], tiles[1], tiles[2][:, 0:64]], axis=1).astype(bf16)
            return carry

        lax.fori_loop(0, RB, one, 0)

    last(zs_even, RB)
    last(zs_odd, 0)
    red_copy = pltpu.make_async_copy(rbuf, red_hbm, sem_out.at[1])
    red_copy.start()
    for ref, sem in pending_sends:
        pltpu.make_async_copy(ref, ref, sem).wait()
    feat_copy.wait()
    red_copy.wait()


def hand_over(feat_from, red_from, feat_to, red_to, feat_buf, red_buf, sem_from, sem_to):
    step = TH // 4
    moves = [(feat_from.at[pl.ds(step * i, step)], feat_buf.at[pl.ds(step * i, step)], feat_to.at[pl.ds(step * i, step)]) for i in range(4)]
    moves.append((red_from, red_buf, red_to))
    reads = [pltpu.make_async_copy(a, b, sem_from.at[i]) for i, (a, b, _) in enumerate(moves)]
    writes = [pltpu.make_async_copy(b, c, sem_to.at[i]) for i, (_, b, c) in enumerate(moves)]
    for read in reads:
        read.start()
    for read, write in zip(reads, writes):
        read.wait()
        write.start()
    for write in writes:
        write.wait()


def local(latent, conv_weights, conv_bias, norm_gain, norm_shift, time_shift):
    vmem, anywhere = pl.BlockSpec(memory_space=pltpu.VMEM), pl.BlockSpec(memory_space=pl.ANY)
    results = (
        jax.ShapeDtypeStruct((TH, TW, C), bf16),
        jax.ShapeDtypeStruct((TH // 2, TW // 2, C), bf16),
    )
    features, reduced = pl.pallas_call(
        kernel,
        out_shape=results,
        in_specs=[anywhere, anywhere, vmem, vmem, vmem, vmem],
        out_specs=(anywhere, anywhere),
        scratch_shapes=[
            pltpu.VMEM((TH, TW, C), bf16),
            pltpu.VMEM((5, SHARD, C), bf16),
            pltpu.VMEM((TH + 2, TW, 384), bf16),
            pltpu.VMEM((TH + 2, TW, 384), bf16),
            pltpu.VMEM((TH + 2, TW, 384), bf16),
            pltpu.VMEM((TH + 2, TW, 128), bf16),
            pltpu.VMEM((2 * TH, 1024), bf16),
            pltpu.VMEM((8, RB, 80, 128), f32),
            pltpu.VMEM((8, RB, 80, 128), f32),
            pltpu.VMEM((5, 2, 3, 48, 128), f32),
            pltpu.VMEM((2, 3, 48, 128), f32),
            pltpu.VMEM((5, 2, 3, TH, 128), f32),
            pltpu.VMEM((5, 2, NR, 240, 128), bf16),
            pltpu.VMEM((2, 1024, 1024), bf16),
            pltpu.VMEM((384, 128), bf16),
            pltpu.VMEM((128, 384), bf16),
            pltpu.VMEM((6, 1, 128), f32),
            pltpu.VMEM((4, NR * NCOL - 1, 1, 128), f32),
            pltpu.VMEM((NR + NCOL - 2, 1, 128), f32),
            pltpu.VMEM((TH, TW, C), bf16),
            pltpu.VMEM((TH // 2, TW // 2, C), bf16),
            pltpu.SemaphoreType.DMA((5,)),
            pltpu.SemaphoreType.DMA((2,)),
            pltpu.SemaphoreType.DMA((5, 3)),
            pltpu.SemaphoreType.DMA((5, 3)),
            pltpu.SemaphoreType.DMA((5, 8)),
            pltpu.SemaphoreType.DMA((5, 8)),
            pltpu.SemaphoreType.DMA((6,)),
            pltpu.SemaphoreType.DMA((6,)),
        ],
        compiler_params=pltpu.CompilerParams(
            collective_id=0, has_side_effects=True, vmem_limit_bytes=60 * 1024 * 1024
        ),
        name="down_block",
    )(latent, conv_weights, conv_bias, norm_gain, norm_shift, time_shift)
    return pl.pallas_call(
        hand_over,
        out_shape=results,
        in_specs=[anywhere, anywhere],
        out_specs=(anywhere, anywhere),
        scratch_shapes=[
            pltpu.VMEM((TH, TW, C), bf16),
            pltpu.VMEM((TH // 2, TW // 2, C), bf16),
            pltpu.SemaphoreType.DMA((5,)),
            pltpu.SemaphoreType.DMA((5,)),
        ],
        name="hand_over",
    )(features, reduced)


def solution(mesh):
    split = Mesh(mesh.devices.reshape(NY, NX, NZ, NC), ("rows_0", "rows_1", "cols_0", "cols_1"))
    placed = (P(ROWS, COLS, None), P(None, ROWS, None), P(), P(), P(), P())
    return jax.shard_map(
        local,
        mesh=split,
        in_specs=placed,
        out_specs=(P(ROWS, COLS, None), P(ROWS, COLS, None)),
        check_vma=False,
    )
```

```python
import functools
import itertools

import jax
import jax.numpy as jnp
from jax import lax
from jax.experimental import pallas as pl
from jax.experimental.pallas import tpu as pltpu
from jax.sharding import Mesh
from jax.sharding import PartitionSpec as P

f32, bf16 = jnp.float32, jnp.bfloat16
MESH = pl.DeviceIdType.MESH
ROWS = ("rows_0", "rows_1")
COLS = ("cols_0", "cols_1")
NY, NX, NZ, NC = 4, 4, 4, 2
NR, NCOL = NY * NX, NZ * NC
C = 320
TH, TW = 32, 64
SHARD = 180
RB = 8
NB = TH // RB
EPS = 1e-05


def padded(row, width=384):
    return jnp.concatenate([row, jnp.zeros((row.shape[0], width - row.shape[1]), row.dtype)], axis=1)


def window_tiles():
    tiles = []
    for tile in range(9 * C // 16):
        holders = []
        for r in range(NR):
            first = SHARD * r // 16
            last = (SHARD * (r + 1) - 1) // 16
            if first <= tile <= last:
                holders.append((r, tile - first))
        tiles.append(holders)
    return tiles


WINDOWS = window_tiles()


def others():
    sizes = (NY, NX, NZ, NC)
    steps = [o for o in itertools.product(*[range(n) for n in sizes]) if any(o)]
    return sorted(steps, key=lambda o: -sum(2 * min(v, n - v) for v, n in zip(o[:3], sizes)) - o[3])


OTHERS = others()


def kernel(
    lat_hbm, w_hbm, bias_ref, gain_ref, shift_ref, time_ref,
    feat_hbm, red_hbm,
    lat, wl, act_a, act_b, xs, r0, edge_mat, zs_even, zs_odd, hc, es, cs, gath, wk, to_group, to_channel,
    ar_src, ar_got, ar_first, fbuf, rbuf,
    sem_in, sem_out, ws_send, ws_recv, halo_send, halo_recv, ar_send, ar_recv,
):
    y, x = lax.axis_index("rows_0"), lax.axis_index("rows_1")
    z, core = lax.axis_index("cols_0"), lax.axis_index("cols_1")
    r, c = y * NX + x, z * NC + core

    def dev(rr, cc):
        return (rr // NX, lax.rem(rr, NX), cc // NC, lax.rem(cc, NC))

    def row_peer(j):
        return dev(lax.rem(r + j, NR), c)

    def col_peer(j):
        return dev(r, lax.rem(c + j, NCOL))

    up, down = lax.rem(r + NR - 1, NR), lax.rem(r + 1, NR)
    left, right = lax.rem(c + NCOL - 1, NCOL), lax.rem(c + 1, NCOL)

    lat_copies = []
    for i in range(4):
        cp = pltpu.make_async_copy(lat_hbm.at[pl.ds(8 * i, 8)], lat.at[pl.ds(8 * i, 8)], sem_in.at[i])
        cp.start()
        lat_copies.append(cp)
    w_copy = pltpu.make_async_copy(w_hbm, wl, sem_in.at[4])
    w_copy.start()

    barrier = pltpu.get_barrier_semaphore()
    peers = [row_peer(j) for j in range(1, NR)] + [col_peer(j) for j in range(1, NCOL)]
    for peer in peers:
        pl.semaphore_signal(barrier, inc=1, device_id=peer, device_id_type=MESH)

    major = jnp.where(core == 0, y, x)
    minor = jnp.where(core == 0, x, y)
    slot = 4 * major + minor
    w_copy.wait()
    off = lax.rem(4 * r, 16)
    row_id = lax.broadcasted_iota(jnp.int32, (96, SHARD), 0) + 96 * core
    col_id = lax.broadcasted_iota(jnp.int32, (96, SHARD), 1) + off
    place = jnp.where(row_id == col_id, 1.0, 0.0).astype(bf16)

    def prepare(k):
        half = jnp.dot(place, wl[k], preferred_element_type=f32)
        gath[k, core, slot, 0:96] = half[:, 0:128].astype(bf16)
        gath[k, core, slot, 96:192] = half[:, 128:256].astype(bf16)
        tail = jnp.concatenate([half[0:48, 256:320], half[48:96, 256:320]], axis=1)
        gath[k, core, slot, 192:240] = tail.astype(bf16)

    prepare(0)
    ci = lax.broadcasted_iota(jnp.int32, (384, 128), 0)
    gi = lax.broadcasted_iota(jnp.int32, (384, 128), 1)
    to_group[...] = jnp.where(((ci * 6554) >> 16) == gi, 1.0, 0.0).astype(bf16)
    ci = lax.broadcasted_iota(jnp.int32, (128, 384), 1)
    gi = lax.broadcasted_iota(jnp.int32, (128, 384), 0)
    to_channel[...] = jnp.where(((ci * 6554) >> 16) == gi, 1.0, 0.0).astype(bf16)


    def along(step_minor, step_major):
        mi = lax.rem(minor + step_minor, 4)
        ma = lax.rem(major + step_major, 4)
        return (jnp.where(core == 0, ma, mi), jnp.where(core == 0, mi, ma), z, core)

    pending_sends = []

    def w_stage1(k):
        mine = gath.at[k, core, slot]
        for j in range(1, 4):
            pltpu.make_async_remote_copy(mine, mine, ws_send.at[k, 0], ws_recv.at[k, 0], along(j, 0), MESH).start()
        pending_sends.append((gath.at[k, 0, 0:3], ws_send.at[k, 0]))

    def w_stage2(k):
        three = gath.at[k, 0, 0:3]
        pltpu.make_async_copy(three, three, ws_recv.at[k, 0]).wait()
        mine = gath.at[k, core, pl.ds(4 * major, 4)]
        for j in range(1, 4):
            pltpu.make_async_remote_copy(mine, mine, ws_send.at[k, 1], ws_recv.at[k, 1], along(0, j), MESH).start()
        pending_sends.append((gath.at[k, 0, 0:12], ws_send.at[k, 1]))

    def w_swap(k):
        twelve = gath.at[k, 0, 0:12]
        pltpu.make_async_copy(twelve, twelve, ws_recv.at[k, 1]).wait()
        mine = gath.at[k, core]
        pltpu.make_async_remote_copy(
            mine, mine, ws_send.at[k, 2], ws_recv.at[k, 2], (y, x, z, 1 - core), MESH
        ).start()
        pending_sends.append((gath.at[k, 0], ws_send.at[k, 2]))

    def w_arrived(k):
        every = gath.at[k, 0]
        pltpu.make_async_copy(every, every, ws_recv.at[k, 2]).wait()


    lane = lax.broadcasted_iota(jnp.int32, (1, 128), 1)
    low = lane < 64

    def relayout(k):
        wbuf = wk.at[k % 2]

        def piece(holder, part):
            rr, l = holder
            h, l6 = l // 6, l % 6
            s = rr if h == 0 else (rr % NX) * NY + rr // NX
            if part < 2:
                return gath[k, h, s, 96 * part + 16 * l6 : 96 * part + 16 * l6 + 16]
            t = gath[k, h, s, 192 + 16 * (l6 % 3) : 208 + 16 * (l6 % 3)].astype(f32)
            return t if l6 < 3 else pltpu.roll(t, 64, 1)

        def tile(t, part):
            return functools.reduce(lambda p, q: p + q, [piece(h, part) for h in WINDOWS[t]])

        for a in range(3):
            for u in range(20):
                row = 256 * a + 16 * u if u < 16 else 768 + 64 * a + 16 * (u - 16)
                tails = []
                for b in range(3):
                    t = 20 * (3 * a + b) + u
                    for part in range(2):
                        wbuf[row : row + 16, 256 * b + 128 * part : 256 * b + 128 * part + 128] = tile(t, part)
                    tails.append(jnp.where(low, tile(t, 2), 0.0))
                wbuf[row : row + 16, 768:896] = (tails[0] + pltpu.roll(tails[1], 64, 1)).astype(bf16)
                wbuf[row : row + 16, 896:1024] = tails[2].astype(bf16)

    zero_acc = tuple(jnp.zeros((8, 128), f32) for _ in range(6))

    def fold(v):
        return jnp.sum(v.reshape(v.shape[0] // 8, 8, 128), axis=0)

    def add_stats(acc, tiles):
        sums = [acc[t] + fold(tiles[t]) for t in range(3)]
        squares = [acc[3 + t] + fold(tiles[t] * tiles[t]) for t in range(3)]
        return tuple(sums + squares)

    def stage_cols(phase, row, tiles):
        for t in range(3):
            cs[phase, 0, t, pl.ds(row, 1), :] = tiles[t][0:1]
            cs[phase, 1, t, pl.ds(row, 1), :] = tiles[t][63:64]

    def halo_messages(phase, act):
        msgs = [
            (act.at[TH], act.at[0], dev(down, c)),
            (cs.at[phase, 1], hc.at[phase, 0, :, 8:40, :], dev(r, right)),
            (cs.at[phase, 1, :, 24:32, :], hc.at[phase, 0, :, 0:8, :], dev(down, right)),
        ]
        if phase < 4:
            msgs += [
                (act.at[1], act.at[TH + 1], dev(up, c)),
                (cs.at[phase, 0], hc.at[phase, 1, :, 8:40, :], dev(r, left)),
                (cs.at[phase, 0, :, 24:32, :], hc.at[phase, 1, :, 0:8, :], dev(down, left)),
                (cs.at[phase, 1, :, 0:8, :], hc.at[phase, 0, :, 40:48, :], dev(up, right)),
                (cs.at[phase, 0, :, 0:8, :], hc.at[phase, 1, :, 40:48, :], dev(up, left)),
            ]
        return [
            pltpu.make_async_remote_copy(s, d, halo_send.at[phase, i], halo_recv.at[phase, i], to, MESH)
            for i, (s, d, to) in enumerate(msgs)
        ]

    def thirds(v):
        hi = v.astype(bf16).astype(f32)
        mid = (v - hi).astype(bf16).astype(f32)
        return jnp.concatenate([hi, mid, v - hi - mid], axis=0).astype(bf16)

    def own_sums(acc):
        sums = jnp.concatenate(
            [jnp.concatenate(acc[0:3], axis=1), jnp.concatenate(acc[3:6], axis=1)], axis=0
        )
        got = jnp.dot(thirds(sums), to_group[...], preferred_element_type=f32)
        got = got[0:16] + got[16:32] + got[32:48]
        return jnp.sum(got[0:8], axis=0, keepdims=True) + pltpu.roll(jnp.sum(got[8:16], axis=0, keepdims=True), 32, 1)

    def send_sums(phase, own):
        ar_src[phase] = own
        me = (y, x, z, core)
        for j, offset in enumerate(OTHERS):
            to = tuple(lax.rem(m + o, n) if o else m for m, o, n in zip(me, offset, (NY, NX, NZ, NC)))
            pltpu.make_async_remote_copy(
                ar_src.at[phase], ar_got.at[phase, j], ar_send.at[phase], ar_recv.at[phase], to, MESH
            ).start()
        pending_sends.append((ar_got.at[phase], ar_send.at[phase]))

    def first_sums(own, between):
        at = 0
        for stage, (peer, n) in enumerate(((col_peer, NCOL), (row_peer, NR))):
            ar_src[4 + stage] = own
            got = ar_first.at[pl.ds(at, n - 1)]
            for j in range(1, n):
                pltpu.make_async_remote_copy(
                    ar_src.at[4 + stage], ar_first.at[at + j - 1], ar_send.at[4 + stage], ar_recv.at[4 + stage], peer(j), MESH
                ).start()
            pending_sends.append((got, ar_send.at[4 + stage]))
            between[stage]()
            pltpu.make_async_copy(got, got, ar_recv.at[4 + stage]).wait()
            own = own + jnp.sum(ar_first[at : at + n - 1], axis=0)
            at += n - 1
        return own

    def all_sums(phase, own):
        every = ar_got.at[phase]
        pltpu.make_async_copy(every, every, ar_recv.at[phase]).wait()
        return own + jnp.sum(ar_got[phase], axis=0)

    def scales(phase, vec):
        count = float(TH * NR * TW * NCOL * (C // 32))
        mean = vec / count
        spread = jnp.maximum(pltpu.roll(mean, 96, 1) - mean * mean, 0.0)
        scale = lax.rsqrt(spread + EPS)
        pair = jnp.concatenate([scale, mean * scale], axis=0)
        pair = jnp.where(lane < 32, pair, 0.0)
        tot = jnp.dot(thirds(jnp.concatenate([pair, jnp.zeros((6, 128), f32)], axis=0)), to_channel[...], preferred_element_type=f32)
        tot = tot[0:8] + tot[8:16] + tot[16:24]
        gain = padded(0.5 * gain_ref[phase : phase + 1, :])
        scale = tot[0:1] * gain
        move = padded(0.5 * shift_ref[phase : phase + 1, :]) - tot[1:2] * gain
        return [scale[:, 128 * t : 128 * t + 128] for t in range(3)], [move[:, 128 * t : 128 * t + 128] for t in range(3)]

    def silu_of(v, scale, move):
        half = v * scale + move
        return half + half * jnp.tanh(half)

    def on(cond):
        return jnp.where(cond, 1.0, 0.0).astype(f32)

    top, bottom = on(r > 0), on(r < NR - 1)
    west, east = on(c > 0), on(c < NCOL - 1)

    def edge_taps(side, rows, stride):
        def tap(t, a):
            if stride > 1:
                return es[side, t, pl.ds(7 + a, rows, stride=stride), :]
            return es[side, t, 7 + a : 7 + a + rows, :]

        cols = [tap(t, a) for a in range(3) for t in range(2)]
        return cols + [tap(2, 0) + pltpu.roll(tap(2, 1), 64, 1), tap(2, 2)]

    def edges_to_matrix():
        both = [edge_taps(side, TH, 1) for side in range(2)]
        for b in range(NB):
            for i in range(8):
                pair = [both[side][i][RB * b : RB * b + RB] for side in range(2)]
                edge_mat[2 * RB * b : 2 * RB * (b + 1), 128 * i : 128 * i + 128] = jnp.concatenate(pair, axis=0).astype(bf16)

    er = lax.broadcasted_iota(jnp.int32, (48, 1), 0)
    edge_rows = jnp.where(er < 8, top, jnp.where(er < 40, 1.0, bottom))

    def norm_rows(act, sc, mv, carry, rows):
        for i in reversed(rows):
            tiles = []
            for t in range(3):
                scale, move = sc[t], mv[t]
                if i in (0, TH + 1):
                    mask = top if i == 0 else bottom
                    scale, move = scale * mask, move * mask
                v = act[i, :, 128 * t : 128 * t + 128].astype(f32)
                tiles.append(silu_of(v, scale, move))
                xs[i, :, 128 * t : 128 * t + 128] = tiles[t].astype(bf16)
            if carry[0] is not None:
                r0[i + 1] = (tiles[2] + carry[0]).astype(bf16)
            carry[0] = pltpu.roll(tiles[2], 64, 1)

    def norm_edges(phase, sc, mv):
        for side, mask in ((0, west), (1, east)):
            for t in range(3):
                es[side, t] = silu_of(hc[phase, side, t], sc[t], mv[t]) * (edge_rows * mask)
        edges_to_matrix()

    def block_dot(k, zs, parts, edges, work):
        lhs = jnp.concatenate([jnp.concatenate(parts, axis=1), edges], axis=0)
        rows = RB * TW
        for n in range(4):
            o = jnp.dot(lhs, wk[k % 2, :, 256 * n : 256 * n + 256], preferred_element_type=f32)
            for t in range(2):
                p = o[:, 128 * t : 128 * t + 128]
                tile = 2 * n + t
                zs[tile, :, 8 : 8 + TW, :] = p[0:rows].reshape(RB, TW, 128)
                if tile in (0, 1, 6):
                    for rr in range(RB):
                        zs[tile, rr, 7:8, :] = p[rows + rr : rows + rr + 1]
                if tile in (4, 5, 7):
                    for rr in range(RB):
                        zs[tile, rr, 8 + TW : 9 + TW, :] = p[rows + RB + rr : rows + RB + rr + 1]
            for item in work[len(work) * n // 4 : len(work) * (n + 1) // 4]:
                item()

    def taps_sum(zs, rr, width, stride):
        def at(t, first):
            if stride > 1:
                return zs[t, rr, pl.ds(first, width, stride=stride), :]
            return zs[t, rr, first : first + width, :]

        outs = [at(t, 7) + at(2 + t, 8) + at(4 + t, 9) for t in range(2)]
        tail = at(6, 7) + pltpu.roll(at(6, 8), 64, 1) + at(7, 9)
        return outs + [jnp.where(low, tail, 0.0)]

    def split(row):
        row = padded(row)
        return [row[:, 128 * t : 128 * t + 128] for t in range(3)]

    def convolve(k, act, sc, mv, res, out, ahead, hooks):
        extra = split(bias_ref[k : k + 1, :] + (time_ref[k // 2 : k // 2 + 1, :] if k % 2 == 0 else 0.0))
        stats = [zero_acc]
        carry = [None]

        def norm_item(rows):
            return lambda: norm_rows(act, sc, mv, carry, rows)

        def needed(b):
            return range(RB * b, RB * b + RB if b < NB - 1 else TH + 2)

        def finish_row(zs, b, rr):
            row = RB * b + rr
            tiles = []
            for t, o in enumerate(taps_sum(zs, rr, TW, 1)):
                o = o + extra[t]
                if res is not None:
                    o = o + res[row + 1, :, 128 * t : 128 * t + 128].astype(f32)
                o = o.astype(bf16)
                out[row + 1, :, 128 * t : 128 * t + 128] = o
                tiles.append(o.astype(f32))
            for t in range(3):
                cs[k + 1, 0, t, row : row + 1, :] = tiles[t][0:1]
                cs[k + 1, 1, t, row : row + 1, :] = tiles[t][TW - 1 : TW]
            if k == 3:
                fbuf[row] = jnp.concatenate([tiles[0], tiles[1], tiles[2][:, 0:64]], axis=1).astype(bf16)
            else:
                stats[0] = add_stats(stats[0], tiles)

        def finish_item(zs, b, rr):
            return lambda: finish_row(zs, b, rr)

        norm_rows(act, sc, mv, carry, needed(NB - 1))
        if ahead is not None:
            ahead[0]()
            norm_rows(act, sc, mv, carry, needed(NB - 2))
            ahead[1]()
        before = []
        for step, b in enumerate(reversed(range(NB))):
            zs = zs_even if step % 2 == 0 else zs_odd
            if step in hooks:
                hooks[step]()
            parts = [xs[RB * b + a : RB * b + a + RB, :, 0:256].reshape(RB * TW, 256) for a in range(3)]
            parts.append(r0[RB * b + 1 : RB * b + 1 + RB].reshape(RB * TW, 128))
            parts.append(xs[RB * b + 2 : RB * b + 2 + RB, :, 256:384].reshape(RB * TW, 128))
            work = list(before)
            later = b - 1 if ahead is None else b - 2
            if later >= 0:
                norms = [norm_item(range(i, i + 1)) for i in reversed(needed(later))]
                work = [w for pair in itertools.zip_longest(norms, work) for w in pair if w is not None]
            block_dot(k, zs, parts, edge_mat[2 * RB * b : 2 * RB * (b + 1)], work)
            before = [finish_item(zs, b, rr) for rr in reversed(range(RB))]
        for item in before:
            item()
        return stats[0]

    def read_latent(i, acc):
        v = lat[i].astype(f32)
        tiles = [v[:, 0:128], v[:, 128:256], padded(v[:, 256:320], 128)]
        for t in range(3):
            act_a[i + 1, :, 128 * t : 128 * t + 128] = tiles[t].astype(bf16)
        stage_cols(0, i, tiles)
        return add_stats(acc, tiles)

    acc = zero_acc
    for i in range(4):
        lat_copies[i].wait()
        acc = lax.fori_loop(8 * i, 8 * i + 8, read_latent, acc)


    pl.semaphore_wait(barrier, len(peers))
    w_stage1(0)

    for k in range(4):
        act, res, out = (act_a, None, act_b) if k % 2 == 0 else (act_b, act_a, act_a)
        own = own_sums(acc)
        halos = halo_messages(k, act)
        straight = [h for i, h in enumerate(halos) if i in (0, 1, 3, 4)]
        corners = [h for i, h in enumerate(halos) if i in (2, 5, 6, 7)]
        ahead = None
        if k == 0:
            def beside_first():
                for h in straight:
                    h.start()
                for later in range(1, 5):
                    prepare(later)
                for i in range(2):
                    wk[i, 960:1024, :] = jnp.zeros((64, 1024), bf16)

            def beside_second():
                for h in corners:
                    h.start()
                w_stage2(0)
                w_stage1(1)

            def got_first():
                w_arrived(0)
                w_stage2(1)
                relayout(0)

            ahead = (functools.partial(w_swap, 0), got_first)
            total = first_sums(own, (beside_first, beside_second))
        else:
            send_sums(k, own)
            for h in straight + corners:
                h.start()
            w_swap(k)
            if k == 3:
                w_stage2(4)
            else:
                w_stage1(k + 1)
                if k == 2:
                    w_stage1(4)
            w_arrived(k)
            relayout(k)
            total = all_sums(k, own)
        sc, mv = scales(k, total)
        for h in halos:
            h.wait()
        norm_edges(k, sc, mv)
        hooks = {}
        if k in (1, 2):
            w_stage2(k + 1)
        if k == 3:
            last_halos = halo_messages(4, act_a)

            def lowest_row_done():
                last_halos[0].start()
                last_halos[2].start()

            def last_weights():
                w_arrived(4)
                relayout(4)

            hooks = {1: functools.partial(w_swap, 4), 2: lowest_row_done, 3: last_weights}
        acc = convolve(k, act, sc, mv, res, out, ahead, hooks)

    last_halos[1].start()
    feat_copy = pltpu.make_async_copy(fbuf, feat_hbm, sem_out.at[0])
    feat_copy.start()
    half = TH // 2
    extra4 = split(bias_ref[4:5, :])

    def reduced_parts(b):
        def every_other(first, lanes):
            return jnp.concatenate([act_a[2 * p + first, :, lanes] for p in range(RB * b, RB * b + RB)], axis=0)

        heads = [every_other(a, slice(0, 256)) for a in range(3)]
        pair = every_other(0, slice(256, 384)).astype(f32) + pltpu.roll(every_other(1, slice(256, 384)).astype(f32), 64, 1)
        return heads + [pair.astype(bf16), every_other(2, slice(256, 384))]

    def dot4(zs, parts, edges):
        lhs = jnp.concatenate(parts, axis=1)
        rows = RB * TW
        if edges is not None:
            lhs = jnp.concatenate([lhs, edges], axis=0)
        for n in range(4):
            o = jnp.dot(lhs, wk[0, :, 256 * n : 256 * n + 256], preferred_element_type=f32)
            for t in range(2):
                tile = 2 * n + t
                p = o[:, 128 * t : 128 * t + 128]
                zs[tile, :, 8 : 8 + TW, :] = p[0:rows].reshape(RB, TW, 128)
                if edges is not None and tile in (0, 1, 6):
                    for rr in range(half):
                        (zs_odd if rr < RB else zs_even)[tile, rr % RB, 7:8, :] = p[rows + rr : rows + rr + 1]

    dot4(zs_even, reduced_parts(1), None)
    for h in last_halos:
        h.wait()
    for t in range(3):
        act_a[0, :, 128 * t : 128 * t + 128] = (act_a[0, :, 128 * t : 128 * t + 128].astype(f32) * top).astype(bf16)
        es[0, t] = hc[4, 0, t] * (edge_rows * west)
    left_taps = jnp.concatenate(edge_taps(0, half, 2), axis=1).astype(bf16)
    dot4(zs_odd, reduced_parts(0), left_taps)

    def last(zs, first):
        def one(p, carry):
            tiles = [o + extra4[t] for t, o in enumerate(taps_sum(zs, p, TW // 2, 2))]
            rbuf[first + p] = jnp.concatenate([tiles[0], tiles[1], tiles[2][:, 0:64]], axis=1).astype(bf16)
            return carry

        lax.fori_loop(0, RB, one, 0)

    last(zs_even, RB)
    last(zs_odd, 0)
    red_copy = pltpu.make_async_copy(rbuf, red_hbm, sem_out.at[1])
    red_copy.start()
    for ref, sem in pending_sends:
        pltpu.make_async_copy(ref, ref, sem).wait()
    feat_copy.wait()
    red_copy.wait()


def hand_over(feat_from, red_from, feat_to, red_to, feat_buf, red_buf, sem_from, sem_to):
    step = TH // 4
    moves = [(feat_from.at[pl.ds(step * i, step)], feat_buf.at[pl.ds(step * i, step)], feat_to.at[pl.ds(step * i, step)]) for i in range(4)]
    moves.append((red_from, red_buf, red_to))
    reads = [pltpu.make_async_copy(a, b, sem_from.at[i]) for i, (a, b, _) in enumerate(moves)]
    writes = [pltpu.make_async_copy(b, c, sem_to.at[i]) for i, (_, b, c) in enumerate(moves)]
    for read in reads:
        read.start()
    for read, write in zip(reads, writes):
        read.wait()
        write.start()
    for write in writes:
        write.wait()


def local(latent, conv_weights, conv_bias, norm_gain, norm_shift, time_shift):
    vmem, anywhere = pl.BlockSpec(memory_space=pltpu.VMEM), pl.BlockSpec(memory_space=pl.ANY)
    results = (
        jax.ShapeDtypeStruct((TH, TW, C), bf16),
        jax.ShapeDtypeStruct((TH // 2, TW // 2, C), bf16),
    )
    features, reduced = pl.pallas_call(
        kernel,
        out_shape=results,
        in_specs=[anywhere, anywhere, vmem, vmem, vmem, vmem],
        out_specs=(anywhere, anywhere),
        scratch_shapes=[
            pltpu.VMEM((TH, TW, C), bf16),
            pltpu.VMEM((5, SHARD, C), bf16),
            pltpu.VMEM((TH + 2, TW, 384), bf16),
            pltpu.VMEM((TH + 2, TW, 384), bf16),
            pltpu.VMEM((TH + 2, TW, 384), bf16),
            pltpu.VMEM((TH + 2, TW, 128), bf16),
            pltpu.VMEM((2 * TH, 1024), bf16),
            pltpu.VMEM((8, RB, 80, 128), f32),
            pltpu.VMEM((8, RB, 80, 128), f32),
            pltpu.VMEM((5, 2, 3, 48, 128), f32),
            pltpu.VMEM((2, 3, 48, 128), f32),
            pltpu.VMEM((5, 2, 3, TH, 128), f32),
            pltpu.VMEM((5, 2, NR, 240, 128), bf16),
            pltpu.VMEM((2, 1024, 1024), bf16),
            pltpu.VMEM((384, 128), bf16),
            pltpu.VMEM((128, 384), bf16),
            pltpu.VMEM((6, 1, 128), f32),
            pltpu.VMEM((4, NR * NCOL - 1, 1, 128), f32),
            pltpu.VMEM((NR + NCOL - 2, 1, 128), f32),
            pltpu.VMEM((TH, TW, C), bf16),
            pltpu.VMEM((TH // 2, TW // 2, C), bf16),
            pltpu.SemaphoreType.DMA((5,)),
            pltpu.SemaphoreType.DMA((2,)),
            pltpu.SemaphoreType.DMA((5, 3)),
            pltpu.SemaphoreType.DMA((5, 3)),
            pltpu.SemaphoreType.DMA((5, 8)),
            pltpu.SemaphoreType.DMA((5, 8)),
            pltpu.SemaphoreType.DMA((6,)),
            pltpu.SemaphoreType.DMA((6,)),
        ],
        compiler_params=pltpu.CompilerParams(
            collective_id=0, has_side_effects=True, vmem_limit_bytes=60 * 1024 * 1024
        ),
        name="down_block",
    )(latent, conv_weights, conv_bias, norm_gain, norm_shift, time_shift)
    return pl.pallas_call(
        hand_over,
        out_shape=results,
        in_specs=[anywhere, anywhere],
        out_specs=(anywhere, anywhere),
        scratch_shapes=[
            pltpu.VMEM((TH, TW, C), bf16),
            pltpu.VMEM((TH // 2, TW // 2, C), bf16),
            pltpu.SemaphoreType.DMA((5,)),
            pltpu.SemaphoreType.DMA((5,)),
        ],
        name="hand_over",
    )(features, reduced)


def solution(mesh):
    split = Mesh(mesh.devices.reshape(NY, NX, NZ, NC), ("rows_0", "rows_1", "cols_0", "cols_1"))
    placed = (P(ROWS, COLS, None), P(None, ROWS, None), P(), P(), P(), P())
    return jax.shard_map(
        local,
        mesh=split,
        in_specs=placed,
        out_specs=(P(ROWS, COLS, None), P(ROWS, COLS, None)),
        check_vma=False,
    )
```

```python
import functools
import itertools

import jax
import jax.numpy as jnp
from jax import lax
from jax.experimental import pallas as pl
from jax.experimental.pallas import tpu as pltpu
from jax.sharding import Mesh
from jax.sharding import PartitionSpec as P

f32, bf16 = jnp.float32, jnp.bfloat16
MESH = pl.DeviceIdType.MESH
ROWS = ("rows_0", "rows_1")
COLS = ("cols_0", "cols_1")
NY, NX, NZ, NC = 4, 4, 4, 2
NR, NCOL = NY * NX, NZ * NC
C = 320
TH, TW = 32, 64
SHARD = 180
RB = 8
NB = TH // RB
EPS = 1e-05


def padded(row, width=384):
    return jnp.concatenate([row, jnp.zeros((row.shape[0], width - row.shape[1]), row.dtype)], axis=1)


def window_tiles():
    tiles = []
    for tile in range(9 * C // 16):
        holders = []
        for r in range(NR):
            first = SHARD * r // 16
            last = (SHARD * (r + 1) - 1) // 16
            if first <= tile <= last:
                holders.append((r, tile - first))
        tiles.append(holders)
    return tiles


WINDOWS = window_tiles()


def others():
    sizes = (NY, NX, NZ, NC)
    steps = [o for o in itertools.product(*[range(n) for n in sizes]) if any(o)]
    return sorted(steps, key=lambda o: -sum(2 * min(v, n - v) for v, n in zip(o[:3], sizes)) - o[3])


OTHERS = others()


def kernel(
    lat_hbm, w_hbm, bias_ref, gain_ref, shift_ref, time_ref,
    feat_hbm, red_hbm,
    lat, wl, act_a, act_b, xs, r0, edge_mat, zs_even, zs_odd, hc, es, cs, gath, wk, to_group, to_channel,
    ar_src, ar_got, ar_first, fbuf, rbuf,
    sem_in, sem_out, ws_send, ws_recv, halo_send, halo_recv, ar_send, ar_recv,
):
    y, x = lax.axis_index("rows_0"), lax.axis_index("rows_1")
    z, core = lax.axis_index("cols_0"), lax.axis_index("cols_1")
    r, c = y * NX + x, z * NC + core

    def dev(rr, cc):
        return (rr // NX, lax.rem(rr, NX), cc // NC, lax.rem(cc, NC))

    def row_peer(j):
        return dev(lax.rem(r + j, NR), c)

    def col_peer(j):
        return dev(r, lax.rem(c + j, NCOL))

    up, down = lax.rem(r + NR - 1, NR), lax.rem(r + 1, NR)
    left, right = lax.rem(c + NCOL - 1, NCOL), lax.rem(c + 1, NCOL)

    lat_copies = []
    for i in range(4):
        cp = pltpu.make_async_copy(lat_hbm.at[pl.ds(8 * i, 8)], lat.at[pl.ds(8 * i, 8)], sem_in.at[i])
        cp.start()
        lat_copies.append(cp)
    w_copy = pltpu.make_async_copy(w_hbm, wl, sem_in.at[4])
    w_copy.start()

    barrier = pltpu.get_barrier_semaphore()
    peers = [row_peer(j) for j in range(1, NR)] + [col_peer(j) for j in range(1, NCOL)]
    for peer in peers:
        pl.semaphore_signal(barrier, inc=1, device_id=peer, device_id_type=MESH)

    major = jnp.where(core == 0, y, x)
    minor = jnp.where(core == 0, x, y)
    slot = 4 * major + minor
    w_copy.wait()
    off = lax.rem(4 * r, 16)
    row_id = lax.broadcasted_iota(jnp.int32, (96, SHARD), 0) + 96 * core
    col_id = lax.broadcasted_iota(jnp.int32, (96, SHARD), 1) + off
    place = jnp.where(row_id == col_id, 1.0, 0.0).astype(bf16)

    def prepare(k):
        half = jnp.dot(place, wl[k], preferred_element_type=f32)
        gath[k, core, slot, 0:96] = half[:, 0:128].astype(bf16)
        gath[k, core, slot, 96:192] = half[:, 128:256].astype(bf16)
        tail = jnp.concatenate([half[0:48, 256:320], half[48:96, 256:320]], axis=1)
        gath[k, core, slot, 192:240] = tail.astype(bf16)

    prepare(0)
    ci = lax.broadcasted_iota(jnp.int32, (384, 128), 0)
    gi = lax.broadcasted_iota(jnp.int32, (384, 128), 1)
    to_group[...] = jnp.where(((ci * 6554) >> 16) == gi, 1.0, 0.0).astype(bf16)
    ci = lax.broadcasted_iota(jnp.int32, (128, 384), 1)
    gi = lax.broadcasted_iota(jnp.int32, (128, 384), 0)
    to_channel[...] = jnp.where(((ci * 6554) >> 16) == gi, 1.0, 0.0).astype(bf16)


    def along(step_minor, step_major):
        mi = lax.rem(minor + step_minor, 4)
        ma = lax.rem(major + step_major, 4)
        return (jnp.where(core == 0, ma, mi), jnp.where(core == 0, mi, ma), z, core)

    pending_sends = []

    def w_stage1(k):
        mine = gath.at[k, core, slot]
        for j in range(1, 4):
            pltpu.make_async_remote_copy(mine, mine, ws_send.at[k, 0], ws_recv.at[k, 0], along(j, 0), MESH).start()
        pending_sends.append((gath.at[k, 0, 0:3], ws_send.at[k, 0]))

    def w_stage2(k):
        three = gath.at[k, 0, 0:3]
        pltpu.make_async_copy(three, three, ws_recv.at[k, 0]).wait()
        mine = gath.at[k, core, pl.ds(4 * major, 4)]
        for j in range(1, 4):
            pltpu.make_async_remote_copy(mine, mine, ws_send.at[k, 1], ws_recv.at[k, 1], along(0, j), MESH).start()
        pending_sends.append((gath.at[k, 0, 0:12], ws_send.at[k, 1]))

    def w_swap(k):
        twelve = gath.at[k, 0, 0:12]
        pltpu.make_async_copy(twelve, twelve, ws_recv.at[k, 1]).wait()
        mine = gath.at[k, core]
        pltpu.make_async_remote_copy(
            mine, mine, ws_send.at[k, 2], ws_recv.at[k, 2], (y, x, z, 1 - core), MESH
        ).start()
        pending_sends.append((gath.at[k, 0], ws_send.at[k, 2]))

    def to_other_core(k, steps):
        mine = gath.at[k, core, pl.ds(4 * lax.rem(major + steps, 4), 4)]
        pltpu.make_async_remote_copy(
            mine, mine, ws_send.at[k, 2], ws_recv.at[k, 4], (y, x, z, 1 - core), MESH
        ).start()

    def first_stage2(k):
        three = gath.at[k, 0, 0:3]
        pltpu.make_async_copy(three, three, ws_recv.at[k, 0]).wait()
        mine = gath.at[k, core, pl.ds(4 * major, 4)]
        for j in (2, 1, 3):
            pltpu.make_async_remote_copy(mine, mine, ws_send.at[k, 1], ws_recv.at[k, j], along(0, j), MESH).start()
        to_other_core(k, 0)
        pending_sends.append((gath.at[k, 0, 0:12], ws_send.at[k, 1]))

    def first_swap(k):
        for j in (1, 3, 2):
            four = gath.at[k, 0, 0:4]
            pltpu.make_async_copy(four, four, ws_recv.at[k, j]).wait()
            to_other_core(k, 4 - j)
        pending_sends.append((gath.at[k, 0], ws_send.at[k, 2]))

    def w_arrived(k):
        every = gath.at[k, 0]
        pltpu.make_async_copy(every, every, ws_recv.at[k, 4 if k == 0 else 2]).wait()


    lane = lax.broadcasted_iota(jnp.int32, (1, 128), 1)
    low = lane < 64

    def relayout(k):
        wbuf = wk.at[k % 2]

        def piece(holder, part):
            rr, l = holder
            h, l6 = l // 6, l % 6
            s = rr if h == 0 else (rr % NX) * NY + rr // NX
            if part < 2:
                return gath[k, h, s, 96 * part + 16 * l6 : 96 * part + 16 * l6 + 16]
            t = gath[k, h, s, 192 + 16 * (l6 % 3) : 208 + 16 * (l6 % 3)].astype(f32)
            return t if l6 < 3 else pltpu.roll(t, 64, 1)

        def tile(t, part):
            return functools.reduce(lambda p, q: p + q, [piece(h, part) for h in WINDOWS[t]])

        for a in range(3):
            for u in range(20):
                row = 256 * a + 16 * u if u < 16 else 768 + 64 * a + 16 * (u - 16)
                tails = []
                for b in range(3):
                    t = 20 * (3 * a + b) + u
                    for part in range(2):
                        wbuf[row : row + 16, 256 * b + 128 * part : 256 * b + 128 * part + 128] = tile(t, part)
                    tails.append(jnp.where(low, tile(t, 2), 0.0))
                wbuf[row : row + 16, 768:896] = (tails[0] + pltpu.roll(tails[1], 64, 1)).astype(bf16)
                wbuf[row : row + 16, 896:1024] = tails[2].astype(bf16)

    zero_acc = tuple(jnp.zeros((8, 128), f32) for _ in range(6))

    def fold(v):
        return jnp.sum(v.reshape(v.shape[0] // 8, 8, 128), axis=0)

    def add_stats(acc, tiles):
        sums = [acc[t] + fold(tiles[t]) for t in range(3)]
        squares = [acc[3 + t] + fold(tiles[t] * tiles[t]) for t in range(3)]
        return tuple(sums + squares)

    def stage_cols(phase, row, tiles):
        for t in range(3):
            cs[phase, 0, t, pl.ds(row, 1), :] = tiles[t][0:1]
            cs[phase, 1, t, pl.ds(row, 1), :] = tiles[t][63:64]

    def halo_messages(phase, act):
        msgs = [
            (act.at[TH], act.at[0], dev(down, c)),
            (cs.at[phase, 1], hc.at[phase, 0, :, 8:40, :], dev(r, right)),
            (cs.at[phase, 1, :, 24:32, :], hc.at[phase, 0, :, 0:8, :], dev(down, right)),
        ]
        if phase < 4:
            msgs += [
                (act.at[1], act.at[TH + 1], dev(up, c)),
                (cs.at[phase, 0], hc.at[phase, 1, :, 8:40, :], dev(r, left)),
                (cs.at[phase, 0, :, 24:32, :], hc.at[phase, 1, :, 0:8, :], dev(down, left)),
                (cs.at[phase, 1, :, 0:8, :], hc.at[phase, 0, :, 40:48, :], dev(up, right)),
                (cs.at[phase, 0, :, 0:8, :], hc.at[phase, 1, :, 40:48, :], dev(up, left)),
            ]
        return [
            pltpu.make_async_remote_copy(s, d, halo_send.at[phase, i], halo_recv.at[phase, i], to, MESH)
            for i, (s, d, to) in enumerate(msgs)
        ]

    def thirds(v):
        hi = v.astype(bf16).astype(f32)
        mid = (v - hi).astype(bf16).astype(f32)
        return jnp.concatenate([hi, mid, v - hi - mid], axis=0).astype(bf16)

    def own_sums(acc):
        sums = jnp.concatenate(
            [jnp.concatenate(acc[0:3], axis=1), jnp.concatenate(acc[3:6], axis=1)], axis=0
        )
        got = jnp.dot(thirds(sums), to_group[...], preferred_element_type=f32)
        got = got[0:16] + got[16:32] + got[32:48]
        return jnp.sum(got[0:8], axis=0, keepdims=True) + pltpu.roll(jnp.sum(got[8:16], axis=0, keepdims=True), 32, 1)

    def send_sums(phase, own):
        ar_src[phase] = own
        me = (y, x, z, core)
        for j, offset in enumerate(OTHERS):
            to = tuple(lax.rem(m + o, n) if o else m for m, o, n in zip(me, offset, (NY, NX, NZ, NC)))
            pltpu.make_async_remote_copy(
                ar_src.at[phase], ar_got.at[phase, j], ar_send.at[phase], ar_recv.at[phase], to, MESH
            ).start()
        pending_sends.append((ar_got.at[phase], ar_send.at[phase]))

    def first_sums(own, between):
        at = 0
        for stage, (peer, n) in enumerate(((col_peer, NCOL), (row_peer, NR))):
            ar_src[4 + stage] = own
            got = ar_first.at[pl.ds(at, n - 1)]
            for j in range(1, n):
                pltpu.make_async_remote_copy(
                    ar_src.at[4 + stage], ar_first.at[at + j - 1], ar_send.at[4 + stage], ar_recv.at[4 + stage], peer(j), MESH
                ).start()
            pending_sends.append((got, ar_send.at[4 + stage]))
            between[stage]()
            pltpu.make_async_copy(got, got, ar_recv.at[4 + stage]).wait()
            own = own + jnp.sum(ar_first[at : at + n - 1], axis=0)
            at += n - 1
        return own

    def all_sums(phase, own):
        every = ar_got.at[phase]
        pltpu.make_async_copy(every, every, ar_recv.at[phase]).wait()
        return own + jnp.sum(ar_got[phase], axis=0)

    def scales(phase, vec):
        count = float(TH * NR * TW * NCOL * (C // 32))
        mean = vec / count
        spread = jnp.maximum(pltpu.roll(mean, 96, 1) - mean * mean, 0.0)
        scale = lax.rsqrt(spread + EPS)
        pair = jnp.concatenate([scale, mean * scale], axis=0)
        pair = jnp.where(lane < 32, pair, 0.0)
        tot = jnp.dot(thirds(jnp.concatenate([pair, jnp.zeros((6, 128), f32)], axis=0)), to_channel[...], preferred_element_type=f32)
        tot = tot[0:8] + tot[8:16] + tot[16:24]
        gain = padded(0.5 * gain_ref[phase : phase + 1, :])
        scale = tot[0:1] * gain
        move = padded(0.5 * shift_ref[phase : phase + 1, :]) - tot[1:2] * gain
        return [scale[:, 128 * t : 128 * t + 128] for t in range(3)], [move[:, 128 * t : 128 * t + 128] for t in range(3)]

    def silu_of(v, scale, move):
        half = v * scale + move
        return half + half * jnp.tanh(half)

    def on(cond):
        return jnp.where(cond, 1.0, 0.0).astype(f32)

    top, bottom = on(r > 0), on(r < NR - 1)
    west, east = on(c > 0), on(c < NCOL - 1)

    def edge_taps(side, rows, stride):
        def tap(t, a):
            if stride > 1:
                return es[side, t, pl.ds(7 + a, rows, stride=stride), :]
            return es[side, t, 7 + a : 7 + a + rows, :]

        cols = [tap(t, a) for a in range(3) for t in range(2)]
        return cols + [tap(2, 0) + pltpu.roll(tap(2, 1), 64, 1), tap(2, 2)]

    def edges_to_matrix():
        both = [edge_taps(side, TH, 1) for side in range(2)]
        for b in range(NB):
            for i in range(8):
                pair = [both[side][i][RB * b : RB * b + RB] for side in range(2)]
                edge_mat[2 * RB * b : 2 * RB * (b + 1), 128 * i : 128 * i + 128] = jnp.concatenate(pair, axis=0).astype(bf16)

    er = lax.broadcasted_iota(jnp.int32, (48, 1), 0)
    edge_rows = jnp.where(er < 8, top, jnp.where(er < 40, 1.0, bottom))

    def norm_rows(act, sc, mv, carry, rows):
        for i in reversed(rows):
            tiles = []
            for t in range(3):
                scale, move = sc[t], mv[t]
                if i in (0, TH + 1):
                    mask = top if i == 0 else bottom
                    scale, move = scale * mask, move * mask
                v = act[i, :, 128 * t : 128 * t + 128].astype(f32)
                tiles.append(silu_of(v, scale, move))
                xs[i, :, 128 * t : 128 * t + 128] = tiles[t].astype(bf16)
            if carry[0] is not None:
                r0[i + 1] = (tiles[2] + carry[0]).astype(bf16)
            carry[0] = pltpu.roll(tiles[2], 64, 1)

    def norm_edges(phase, sc, mv):
        for side, mask in ((0, west), (1, east)):
            for t in range(3):
                es[side, t] = silu_of(hc[phase, side, t], sc[t], mv[t]) * (edge_rows * mask)
        edges_to_matrix()

    def block_dot(k, zs, parts, edges, work):
        lhs = jnp.concatenate([jnp.concatenate(parts, axis=1), edges], axis=0)
        rows = RB * TW
        for n in range(4):
            o = jnp.dot(lhs, wk[k % 2, :, 256 * n : 256 * n + 256], preferred_element_type=f32)
            for t in range(2):
                p = o[:, 128 * t : 128 * t + 128]
                tile = 2 * n + t
                zs[tile, :, 8 : 8 + TW, :] = p[0:rows].reshape(RB, TW, 128)
                if tile in (0, 1, 6):
                    for rr in range(RB):
                        zs[tile, rr, 7:8, :] = p[rows + rr : rows + rr + 1]
                if tile in (4, 5, 7):
                    for rr in range(RB):
                        zs[tile, rr, 8 + TW : 9 + TW, :] = p[rows + RB + rr : rows + RB + rr + 1]
            for item in work[len(work) * n // 4 : len(work) * (n + 1) // 4]:
                item()

    def taps_sum(zs, rr, width, stride):
        def at(t, first):
            if stride > 1:
                return zs[t, rr, pl.ds(first, width, stride=stride), :]
            return zs[t, rr, first : first + width, :]

        outs = [at(t, 7) + at(2 + t, 8) + at(4 + t, 9) for t in range(2)]
        tail = at(6, 7) + pltpu.roll(at(6, 8), 64, 1) + at(7, 9)
        return outs + [jnp.where(low, tail, 0.0)]

    def split(row):
        row = padded(row)
        return [row[:, 128 * t : 128 * t + 128] for t in range(3)]

    def convolve(k, act, sc, mv, res, out, ahead, hooks):
        extra = split(bias_ref[k : k + 1, :] + (time_ref[k // 2 : k // 2 + 1, :] if k % 2 == 0 else 0.0))
        stats = [zero_acc]
        carry = [None]

        def norm_item(rows):
            return lambda: norm_rows(act, sc, mv, carry, rows)

        def needed(b):
            return range(RB * b, RB * b + RB if b < NB - 1 else TH + 2)

        def finish_row(zs, b, rr):
            row = RB * b + rr
            tiles = []
            for t, o in enumerate(taps_sum(zs, rr, TW, 1)):
                o = o + extra[t]
                if res is not None:
                    o = o + res[row + 1, :, 128 * t : 128 * t + 128].astype(f32)
                o = o.astype(bf16)
                out[row + 1, :, 128 * t : 128 * t + 128] = o
                tiles.append(o.astype(f32))
            for t in range(3):
                cs[k + 1, 0, t, row : row + 1, :] = tiles[t][0:1]
                cs[k + 1, 1, t, row : row + 1, :] = tiles[t][TW - 1 : TW]
            if k == 3:
                fbuf[row] = jnp.concatenate([tiles[0], tiles[1], tiles[2][:, 0:64]], axis=1).astype(bf16)
            else:
                stats[0] = add_stats(stats[0], tiles)

        def finish_item(zs, b, rr):
            return lambda: finish_row(zs, b, rr)

        norm_rows(act, sc, mv, carry, needed(NB - 1))
        if ahead is not None:
            ahead[0]()
            norm_rows(act, sc, mv, carry, needed(NB - 2))
            ahead[1]()
        before = []
        for step, b in enumerate(reversed(range(NB))):
            zs = zs_even if step % 2 == 0 else zs_odd
            if step in hooks:
                hooks[step]()
            parts = [xs[RB * b + a : RB * b + a + RB, :, 0:256].reshape(RB * TW, 256) for a in range(3)]
            parts.append(r0[RB * b + 1 : RB * b + 1 + RB].reshape(RB * TW, 128))
            parts.append(xs[RB * b + 2 : RB * b + 2 + RB, :, 256:384].reshape(RB * TW, 128))
            work = list(before)
            later = b - 1 if ahead is None else b - 2
            if later >= 0:
                norms = [norm_item(range(i, i + 1)) for i in reversed(needed(later))]
                work = [w for pair in itertools.zip_longest(norms, work) for w in pair if w is not None]
            block_dot(k, zs, parts, edge_mat[2 * RB * b : 2 * RB * (b + 1)], work)
            before = [finish_item(zs, b, rr) for rr in reversed(range(RB))]
        for item in before:
            item()
        return stats[0]

    def read_latent(i, acc):
        v = lat[i].astype(f32)
        tiles = [v[:, 0:128], v[:, 128:256], padded(v[:, 256:320], 128)]
        for t in range(3):
            act_a[i + 1, :, 128 * t : 128 * t + 128] = tiles[t].astype(bf16)
        stage_cols(0, i, tiles)
        return add_stats(acc, tiles)

    acc = zero_acc
    for i in range(4):
        lat_copies[i].wait()
        acc = lax.fori_loop(8 * i, 8 * i + 8, read_latent, acc)


    pl.semaphore_wait(barrier, len(peers))
    w_stage1(0)

    for k in range(4):
        act, res, out = (act_a, None, act_b) if k % 2 == 0 else (act_b, act_a, act_a)
        own = own_sums(acc)
        halos = halo_messages(k, act)
        straight = [h for i, h in enumerate(halos) if i in (0, 1, 3, 4)]
        corners = [h for i, h in enumerate(halos) if i in (2, 5, 6, 7)]
        ahead = None
        if k == 0:
            def beside_first():
                for h in straight:
                    h.start()
                for later in range(1, 5):
                    prepare(later)
                for i in range(2):
                    wk[i, 960:1024, :] = jnp.zeros((64, 1024), bf16)

            def beside_second():
                for h in corners:
                    h.start()
                first_stage2(0)
                w_stage1(1)

            def got_first():
                w_arrived(0)
                w_stage2(1)
                relayout(0)

            ahead = (functools.partial(first_swap, 0), got_first)
            total = first_sums(own, (beside_first, beside_second))
        else:
            send_sums(k, own)
            for h in straight + corners:
                h.start()
            w_swap(k)
            if k == 3:
                w_stage2(4)
            else:
                w_stage1(k + 1)
                if k == 2:
                    w_stage1(4)
            w_arrived(k)
            relayout(k)
            total = all_sums(k, own)
        sc, mv = scales(k, total)
        for h in halos:
            h.wait()
        norm_edges(k, sc, mv)
        hooks = {}
        if k in (1, 2):
            w_stage2(k + 1)
        if k == 3:
            last_halos = halo_messages(4, act_a)

            def lowest_row_done():
                last_halos[0].start()
                last_halos[2].start()

            def last_weights():
                w_arrived(4)
                relayout(4)

            hooks = {1: functools.partial(w_swap, 4), 2: lowest_row_done, 3: last_weights}
        acc = convolve(k, act, sc, mv, res, out, ahead, hooks)

    last_halos[1].start()
    feat_copy = pltpu.make_async_copy(fbuf, feat_hbm, sem_out.at[0])
    feat_copy.start()
    half = TH // 2
    extra4 = split(bias_ref[4:5, :])

    def reduced_parts(b):
        def every_other(first, lanes):
            return jnp.concatenate([act_a[2 * p + first, :, lanes] for p in range(RB * b, RB * b + RB)], axis=0)

        heads = [every_other(a, slice(0, 256)) for a in range(3)]
        pair = every_other(0, slice(256, 384)).astype(f32) + pltpu.roll(every_other(1, slice(256, 384)).astype(f32), 64, 1)
        return heads + [pair.astype(bf16), every_other(2, slice(256, 384))]

    def dot4(zs, parts, edges):
        lhs = jnp.concatenate(parts, axis=1)
        rows = RB * TW
        if edges is not None:
            lhs = jnp.concatenate([lhs, edges], axis=0)
        for n in range(4):
            o = jnp.dot(lhs, wk[0, :, 256 * n : 256 * n + 256], preferred_element_type=f32)
            for t in range(2):
                tile = 2 * n + t
                p = o[:, 128 * t : 128 * t + 128]
                zs[tile, :, 8 : 8 + TW, :] = p[0:rows].reshape(RB, TW, 128)
                if edges is not None and tile in (0, 1, 6):
                    for rr in range(half):
                        (zs_odd if rr < RB else zs_even)[tile, rr % RB, 7:8, :] = p[rows + rr : rows + rr + 1]

    dot4(zs_even, reduced_parts(1), None)
    for h in last_halos:
        h.wait()
    for t in range(3):
        act_a[0, :, 128 * t : 128 * t + 128] = (act_a[0, :, 128 * t : 128 * t + 128].astype(f32) * top).astype(bf16)
        es[0, t] = hc[4, 0, t] * (edge_rows * west)
    left_taps = jnp.concatenate(edge_taps(0, half, 2), axis=1).astype(bf16)
    dot4(zs_odd, reduced_parts(0), left_taps)

    def last(zs, first):
        def one(p, carry):
            tiles = [o + extra4[t] for t, o in enumerate(taps_sum(zs, p, TW // 2, 2))]
            rbuf[first + p] = jnp.concatenate([tiles[0], tiles[1], tiles[2][:, 0:64]], axis=1).astype(bf16)
            return carry

        lax.fori_loop(0, RB, one, 0)

    last(zs_even, RB)
    last(zs_odd, 0)
    red_copy = pltpu.make_async_copy(rbuf, red_hbm, sem_out.at[1])
    red_copy.start()
    for ref, sem in pending_sends:
        pltpu.make_async_copy(ref, ref, sem).wait()
    feat_copy.wait()
    red_copy.wait()


def hand_over(feat_from, red_from, feat_to, red_to, feat_buf, red_buf, sem_from, sem_to):
    step = TH // 4
    moves = [(feat_from.at[pl.ds(step * i, step)], feat_buf.at[pl.ds(step * i, step)], feat_to.at[pl.ds(step * i, step)]) for i in range(4)]
    moves.append((red_from, red_buf, red_to))
    reads = [pltpu.make_async_copy(a, b, sem_from.at[i]) for i, (a, b, _) in enumerate(moves)]
    writes = [pltpu.make_async_copy(b, c, sem_to.at[i]) for i, (_, b, c) in enumerate(moves)]
    for read in reads:
        read.start()
    for read, write in zip(reads, writes):
        read.wait()
        write.start()
    for write in writes:
        write.wait()


def local(latent, conv_weights, conv_bias, norm_gain, norm_shift, time_shift):
    vmem, anywhere = pl.BlockSpec(memory_space=pltpu.VMEM), pl.BlockSpec(memory_space=pl.ANY)
    results = (
        jax.ShapeDtypeStruct((TH, TW, C), bf16),
        jax.ShapeDtypeStruct((TH // 2, TW // 2, C), bf16),
    )
    features, reduced = pl.pallas_call(
        kernel,
        out_shape=results,
        in_specs=[anywhere, anywhere, vmem, vmem, vmem, vmem],
        out_specs=(anywhere, anywhere),
        scratch_shapes=[
            pltpu.VMEM((TH, TW, C), bf16),
            pltpu.VMEM((5, SHARD, C), bf16),
            pltpu.VMEM((TH + 2, TW, 384), bf16),
            pltpu.VMEM((TH + 2, TW, 384), bf16),
            pltpu.VMEM((TH + 2, TW, 384), bf16),
            pltpu.VMEM((TH + 2, TW, 128), bf16),
            pltpu.VMEM((2 * TH, 1024), bf16),
            pltpu.VMEM((8, RB, 80, 128), f32),
            pltpu.VMEM((8, RB, 80, 128), f32),
            pltpu.VMEM((5, 2, 3, 48, 128), f32),
            pltpu.VMEM((2, 3, 48, 128), f32),
            pltpu.VMEM((5, 2, 3, TH, 128), f32),
            pltpu.VMEM((5, 2, NR, 240, 128), bf16),
            pltpu.VMEM((2, 1024, 1024), bf16),
            pltpu.VMEM((384, 128), bf16),
            pltpu.VMEM((128, 384), bf16),
            pltpu.VMEM((6, 1, 128), f32),
            pltpu.VMEM((4, NR * NCOL - 1, 1, 128), f32),
            pltpu.VMEM((NR + NCOL - 2, 1, 128), f32),
            pltpu.VMEM((TH, TW, C), bf16),
            pltpu.VMEM((TH // 2, TW // 2, C), bf16),
            pltpu.SemaphoreType.DMA((5,)),
            pltpu.SemaphoreType.DMA((2,)),
            pltpu.SemaphoreType.DMA((5, 3)),
            pltpu.SemaphoreType.DMA((5, 5)),
            pltpu.SemaphoreType.DMA((5, 8)),
            pltpu.SemaphoreType.DMA((5, 8)),
            pltpu.SemaphoreType.DMA((6,)),
            pltpu.SemaphoreType.DMA((6,)),
        ],
        compiler_params=pltpu.CompilerParams(
            collective_id=0, has_side_effects=True, vmem_limit_bytes=60 * 1024 * 1024
        ),
        name="down_block",
    )(latent, conv_weights, conv_bias, norm_gain, norm_shift, time_shift)
    return pl.pallas_call(
        hand_over,
        out_shape=results,
        in_specs=[anywhere, anywhere],
        out_specs=(anywhere, anywhere),
        scratch_shapes=[
            pltpu.VMEM((TH, TW, C), bf16),
            pltpu.VMEM((TH // 2, TW // 2, C), bf16),
            pltpu.SemaphoreType.DMA((5,)),
            pltpu.SemaphoreType.DMA((5,)),
        ],
        name="hand_over",
    )(features, reduced)


def solution(mesh):
    split = Mesh(mesh.devices.reshape(NY, NX, NZ, NC), ("rows_0", "rows_1", "cols_0", "cols_1"))
    placed = (P(ROWS, COLS, None), P(None, ROWS, None), P(), P(), P(), P())
    return jax.shard_map(
        local,
        mesh=split,
        in_specs=placed,
        out_specs=(P(ROWS, COLS, None), P(ROWS, COLS, None)),
        check_vma=False,
    )
```
